256 devices in a mesh: rep: 8 (over x, y_lo), ep: 32 (over y_hi, z, core).
Axes of the slice: x: 4, y: 4 (y_hi: 2, y_lo: 2; y = y_hi * 2 + y_lo), z: 8, core: 2. Of those that a mesh axis runs over, the one named last changes fastest.
Arguments:
- tokens: bfloat16 [2, 32, 8, 4, 4096], P(None, 'ep', 'rep'), may hold values from -6 to 6
- norm_gain: float32 [4096], replicated, may hold values from 0.5 to 1.5
- expert_ids: int32 [2, 32, 8, 4, 8], P(None, 'ep'), may hold values from 0 to 63, all different within a row; in each aligned block of 32 rows (0 to 31, 32 to 63, ..., all dimensions but the last counted through in order) at most 5 rows name the same one
- route_weights: float32 [2, 32, 8, 4, 8], P(None, 'ep'), may hold values from 0.05 to 1
- w_gate: bfloat16 [64, 1536, 4096], P('ep', 'rep'), may hold values from -0.09375 to 0.09375
- w_up: bfloat16 [64, 1536, 4096], P('ep', 'rep'), may hold values from -0.09375 to 0.09375
- w_down: bfloat16 [64, 1536, 4096], P('ep', 'rep'), may hold values from -0.15625 to 0.15625
Outputs:
- mixed: bfloat16 [2, 32, 8, 4, 4096], P(None, 'ep', 'rep')
The draws below stay inside these ranges and needn't reach their ends.
Inputs may be any that keep to these rules, and one draw needn't show every extreme that they name: `expert_ids`: each row names 8 different experts. In each step, among the rows of one index of ep (32 rows, an aligned block), no expert is named by more than 5 rows, a bound that some block reaches.
All inputs are finite; a program needn't handle non-finite values.
Results may differ from the reference program's by a relative error of at most 0.014.
Values may be sent and summed in bfloat16 or wider, within the bound.
No kernel may reach another device: no remote copies, remote signals or barrier semaphores. Data moves between devices by JAX's collectives and lax.ppermute only.
A program may use at most 128 MiB of HBM per device.

```python
import math
import jax
import jax.numpy as jnp
import numpy as np
from jax import lax

D = 4096
F = 1536
TOPK = 8
STEPS = 2
ROWS_DEV = 4
E = 64
FR = 192
TOKENS = 1024
CAP = 5
N_REP = 8
N_EP = 32


def levels(own_key, dims, pieces, smallest, high):
    gain, own = 1.0, jax.random.fold_in(own_key, 6)
    for axis_at, parts in pieces:
        steps = jnp.exp(jax.random.uniform(jax.random.fold_in(own, axis_at), (parts,), jnp.float32, smallest / len(pieces), high / len(pieces)))
        gain = gain * jnp.repeat(steps, dims[axis_at] // parts).reshape([-1 if axis == axis_at else 1 for axis in range(len(dims))])
    return gain


def routed_block(stream_key, own, number, rows, number_of, top, limit, lean):
    order = jax.random.permutation(stream_key, number_of)
    packed, usual = load_shares(number_of, rows * top, limit, lean, True), load_shares(number_of, rows * top, limit, lean, False)
    places = jnp.arange(number_of)

    def named(lengths, offset_by):
        used = int((lengths > 0).sum())
        fixed = max(1, used // 4)
        moved = fixed + (places - fixed + offset_by * (used - fixed)) % max(1, number_of - fixed)
        return jnp.zeros((number_of,), jnp.int32).at[order[jnp.where(places < fixed, places, moved)]].set(jnp.asarray(lengths, jnp.int32))

    lengths = jnp.where(number % 4 == 0, named(packed, number // 4), named(usual, number - number // 4 - 1))
    mixed = jax.random.permutation(jax.random.fold_in(own, 3), number_of)
    source_of, taker = mixed[0:number_of // 2 * 2:2], mixed[1:number_of // 2 * 2:2]
    margin = jnp.minimum(lengths[source_of] - 1, limit - lengths[taker]) // 2
    margin = jnp.where((source_of == order[0]) | (taker == order[0]) | (lengths[taker] == 0), 0, jnp.maximum(margin, 0))
    moved = jax.random.randint(jax.random.fold_in(own, 4), (number_of // 2,), 0, 1 << 20) % (margin + 1)
    lengths = lengths.at[source_of].add(-moved).at[taker].add(moved)
    items = jnp.searchsorted(jnp.cumsum(lengths), jnp.arange(rows * top), side="right").astype(jnp.int32)
    listing = items.reshape(top, rows).T
    listing = listing[jax.random.permutation(jax.random.fold_in(own, 1), rows)]
    offset_by = jax.random.randint(jax.random.fold_in(own, 2), (rows, 1), 0, top)
    return jnp.take_along_axis(listing, (jnp.arange(top)[None, :] + offset_by) % top, axis=1)


def load_shares(count, total, limit, skew, full):
    weights = [(1 << 20) // math.isqrt(grade ** skew) + 1 for grade in range(1, count + 1)]
    largest = limit if full else min(limit, max(-(-total // count), total * weights[0] // sum(weights)))
    least = 1 if total - largest >= count - 1 else 0
    given, spare = [largest] + [least] * (count - 1), total - largest - least * (count - 1)
    while spare > 0:
        free = [i for i in range(1, count) if given[i] < largest] or [i for i in range(1, count) if given[i] < limit]
        whole, left = sum([weights[i] for i in free]), spare
        for i in free:
            extra = min(limit - given[i], max(1, left * weights[i] // whole), spare)
            given[i] = given[i] + extra
            spare = spare - extra
    return np.array(given)


def bell_draw(key, dims, spread, limit, split=(), held_as=jnp.bfloat16):
    loudness = levels(key, dims, split, -0.22, 0.18) if split else 1.0
    result = jax.random.normal(key, dims, jnp.float32) * spread * loudness
    return jnp.minimum(jnp.maximum(result, -limit), limit).astype(held_as)


def setup_inputs(seed: int = 0) -> dict:
    streams_of = jax.random.split(jax.random.key(seed), 8)
    tokens = bell_draw(streams_of[0], (STEPS, N_EP, N_REP, ROWS_DEV, D), 1.0, 6.0, ((1, 32), (2, 8)))
    norm_gain = jnp.clip(1.0 + 0.1 * jax.random.normal(streams_of[1], (D,), jnp.float32), 0.5, 1.5)
    expert_ids_keys = jax.random.split(jax.random.fold_in(streams_of[2], 1), STEPS * N_EP * N_REP * ROWS_DEV // (N_REP * ROWS_DEV))
    expert_ids_turns = jax.random.permutation(jax.random.fold_in(streams_of[2], 3), STEPS * N_EP * N_REP * ROWS_DEV // (N_REP * ROWS_DEV))
    expert_ids = jax.vmap(lambda own, number: routed_block(jax.random.fold_in(streams_of[2], 2), own, number, N_REP * ROWS_DEV, E, TOPK, CAP, 2))(expert_ids_keys, expert_ids_turns).reshape((STEPS, N_EP, N_REP, ROWS_DEV, TOPK))
    route_weights = jnp.clip(jnp.exp(math.log(1.0) - 2.9957323 * jax.random.uniform(streams_of[3], (STEPS, N_EP, N_REP, ROWS_DEV, TOPK), jnp.float32) ** levels(streams_of[3], (STEPS, N_EP, N_REP, ROWS_DEV, TOPK), ((1, 32),), -0.2, 0.2)), 0.05, 1.0)
    w_gate = bell_draw(streams_of[4], (E, F, D), D ** -0.5, 0.09375, ((0, 32), (1, 8)))
    w_up = bell_draw(streams_of[5], (E, F, D), D ** -0.5, 0.09375, ((0, 32), (1, 8)))
    w_down = bell_draw(streams_of[6], (E, F, D), F ** -0.5, 0.15625, ((0, 32), (1, 8)))
    return dict(tokens=tokens, norm_gain=norm_gain, expert_ids=expert_ids, route_weights=route_weights, w_gate=w_gate, w_up=w_up, w_down=w_down)


epsilon = 1e-06

def norm_rows(values, gain_values):
    widened = values.astype(jnp.float32)
    scaled = lax.rsqrt(lax.optimization_barrier(jnp.mean(widened * widened, axis=-1, keepdims=True)) + epsilon)
    return (widened * scaled * gain_values).astype(jnp.bfloat16)

def reference(tokens, norm_gain, expert_ids, route_weights, w_gate, w_up, w_down):
    groups = F // FR
    row_limit = N_EP * CAP
    flat_tokens = tokens.reshape(STEPS, TOKENS, D)
    flat_ids = expert_ids.reshape(STEPS, TOKENS, TOPK)
    flat_weights = route_weights.reshape(STEPS, TOKENS, TOPK)
    outputs = []
    for step_index in range(STEPS):
        normed = norm_rows(flat_tokens[step_index], norm_gain)
        step_weights = flat_weights[step_index]
        shares = step_weights / lax.optimization_barrier(jnp.sum(step_weights, axis=-1, keepdims=True))
        chosen_ids = flat_ids[step_index]

        def add_expert(mixed_sum, expert):
            chosen = chosen_ids == expert
            row_weight = lax.optimization_barrier(jnp.sum(jnp.where(chosen, shares, 0.0), axis=-1))
            picked = jnp.any(chosen, axis=-1)
            where_rows = jnp.nonzero(picked, size=row_limit, fill_value=TOKENS)[0].astype(jnp.int32)
            picked_rows = jnp.take(normed, where_rows, axis=0, mode='clip')
            gate_out = jnp.dot(picked_rows, w_gate[expert].T, preferred_element_type=jnp.float32)
            up_out = jnp.dot(picked_rows, w_up[expert].T, preferred_element_type=jnp.float32)
            hidden = (jax.nn.silu(gate_out) * up_out).astype(jnp.bfloat16)
            group_parts = jnp.einsum('mgf,gfd->mgd', hidden.reshape(row_limit, groups, FR).astype(jnp.float32), w_down[expert].reshape(groups, FR, D).astype(jnp.float32))
            rounded = lax.optimization_barrier(group_parts.astype(jnp.bfloat16))
            expert_out = lax.optimization_barrier(jnp.sum(rounded.astype(jnp.float32), axis=1))
            weights_here = jnp.take(row_weight, where_rows, axis=0, mode='clip')
            mixed_sum = mixed_sum.at[where_rows].add(weights_here[:, None] * expert_out, mode='drop')
            return (mixed_sum, None)
        mixed_sum, unused = lax.scan(add_expert, jnp.zeros((TOKENS, D), jnp.float32), jnp.arange(E, dtype=jnp.int32))
        outputs.append(mixed_sum.astype(jnp.bfloat16))
    return jnp.stack(outputs).reshape(STEPS, N_EP, N_REP, ROWS_DEV, D)
```

```python
import jax
import jax.numpy as jnp
from jax import lax
from jax.experimental import pallas as pl
from jax.experimental.pallas import tpu as pltpu
from jax.sharding import PartitionSpec as P

epsilon = 1e-06

STEPS = 2
N_REP = 8
N_EP = 32
ROWS = 4
D = 4096
FR = 192
LOCAL = 2
EXPERTS = 64
CAP = 5
TOPK = 8
COLS = D // N_REP
LANES = 128
Q = COLS // LANES
SLOTS = LOCAL * CAP
CHUNK = Q * SLOTS
ALL_ROWS = N_REP * STEPS * ROWS
HALF = N_EP * CAP
GROUP = 16
GROUP_ROWS = GROUP * CHUNK
BLOCK = GROUP * CAP


SMEM = pl.BlockSpec(memory_space=pltpu.SMEM)
HBM = pl.BlockSpec(memory_space=pltpu.HBM)
bf16 = jnp.bfloat16
f32 = jnp.float32


def nt(a, b):
    return lax.dot_general(a, b, (((1,), (1,)), ((), ())), preferred_element_type=f32)


def nn(a, b):
    return lax.dot_general(a, b, (((1,), (0,)), ((), ())), preferred_element_type=f32)


def small_div(value, by):
    return (value * ((1 << 20) // by + 1)) >> 20


def whole(shape):
    return pl.BlockSpec(
        shape, lambda index: (0,) * len(shape), pipeline_mode=pl.Buffered(buffer_count=1)
    )


def call(kernel, out_shapes, operands, memory=None, scratch=(), limit=12, hbm=()):
    memory = memory or {}
    many = isinstance(out_shapes, (list, tuple))
    out_specs = [whole(each.shape) for each in out_shapes] if many else whole(out_shapes.shape)
    operands = [
        pltpu.with_memory_space_constraint(each, pltpu.HBM)
        if at in hbm or memory.get(at) is HBM
        else each
        for at, each in enumerate(operands)
    ]
    return pl.pallas_call(
        kernel,
        out_shape=out_shapes,
        grid=(1,),
        in_specs=[memory.get(at, whole(each.shape)) for at, each in enumerate(operands)],
        out_specs=out_specs,
        scratch_shapes=list(scratch),
        compiler_params=pltpu.CompilerParams(vmem_limit_bytes=limit << 20),
    )(*operands)


def norm_kernel(tokens, gain, out):
    parts = []
    for step in range(STEPS):
        widened = tokens[step].astype(f32)
        mean = jnp.mean(widened * widened, axis=-1, keepdims=True)
        parts.append(widened * lax.rsqrt(mean + epsilon) * gain[...])
    both = jnp.concatenate(parts, axis=0).astype(bf16)
    for part in range(N_REP):
        out[part] = both[:, part * COLS : (part + 1) * COLS]


def tables_kernel(ids, weights, send, keep_hi, keep_lo, sort, unsort):
    shares = weights[...] / jnp.sum(weights[...], axis=-1, keepdims=True)
    chosen = ids[...]
    expert = lax.broadcasted_iota(jnp.int32, (ALL_ROWS, EXPERTS), 1)
    member = jnp.zeros((ALL_ROWS, EXPERTS), f32)
    share = jnp.zeros((ALL_ROWS, EXPERTS), f32)
    for which in range(TOPK):
        hit = chosen[:, which : which + 1] == expert
        member = member + jnp.where(hit, 1.0, 0.0)
        share = share + jnp.where(hit, shares[:, which : which + 1], 0.0)
    row = lax.broadcasted_iota(jnp.int32, (ALL_ROWS, ALL_ROWS), 0)
    other = lax.broadcasted_iota(jnp.int32, (ALL_ROWS, ALL_ROWS), 1)
    earlier = (other < row) & (((row >> 2) & 1) == ((other >> 2) & 1))
    position = nn(jnp.where(earlier, 1.0, 0.0).astype(bf16), member.astype(bf16))
    position = jnp.where(member > 0.5, position, 100.0).astype(bf16)
    share_hi = share.astype(bf16)
    share_lo = (share - share_hi.astype(f32)).astype(bf16)
    position = jnp.concatenate([position] * Q, axis=0)
    share_hi = jnp.concatenate([share_hi] * Q, axis=0)
    share_lo = jnp.concatenate([share_lo] * Q, axis=0)

    def split(line, by_target):
        target = small_div(line, by_target)
        rest = line - target * by_target
        step = (rest >= CHUNK).astype(jnp.int32)
        rest = rest - step * CHUNK
        part = small_div(rest, SLOTS)
        slot = rest - part * SLOTS
        local = (slot >= CAP).astype(jnp.int32)
        return target * LOCAL + local, step, part, slot - local * CAP

    wide = 256

    def send_block(index, carry):
        at = pl.multiple_of(index * wide, wide)
        line = lax.broadcasted_iota(jnp.int32, (wide, 1), 0) + at
        bucket, step, part, place = split(line, 2 * CHUNK)
        pick = lax.broadcasted_iota(jnp.int32, (wide, EXPERTS), 1) == bucket
        found = nt(jnp.where(pick, 1.0, 0.0).astype(bf16), position)
        column = lax.broadcasted_iota(jnp.int32, (wide, Q * ALL_ROWS), 1)
        right = (found == place.astype(f32)) & (
            (column >> 6) * 2 + ((column >> 2) & 1) == part * 2 + step
        )
        send[pl.ds(at, wide), :] = jnp.where(right, 1.0, 0.0).astype(bf16)
        return carry

    lax.fori_loop(0, STEPS * N_EP * CHUNK // wide, send_block, 0)

    def keep_block(index, carry):
        at = pl.multiple_of(index * wide, wide)
        line = lax.broadcasted_iota(jnp.int32, (1, wide), 1) + at
        bucket, _, part, place = split(line, CHUNK)
        pick = lax.broadcasted_iota(jnp.int32, (EXPERTS, wide), 0) == bucket
        pick = jnp.where(pick, 1.0, 0.0).astype(bf16)
        found = nn(position, pick)
        high = nn(share_hi, pick)
        low = nn(share_lo, pick)
        line = lax.broadcasted_iota(jnp.int32, (Q * ALL_ROWS, wide), 0)
        right = (found == place.astype(f32)) & ((line >> 6) == part)
        for step in range(STEPS):
            now = right & (((line >> 2) & 1) == step)
            keep_hi[step, :, pl.ds(at, wide)] = jnp.where(now, high, 0.0).astype(bf16)
            keep_lo[step, :, pl.ds(at, wide)] = jnp.where(now, low, 0.0).astype(bf16)
        return carry

    lax.fori_loop(0, N_EP * CHUNK // wide, keep_block, 0)

    def stacked_from(line):
        part = small_div(line, 2 * BLOCK)
        rest = line - part * (2 * BLOCK)
        local = (rest >= BLOCK).astype(jnp.int32)
        rest = rest - local * BLOCK
        source = small_div(rest, CAP)
        place = rest - source * CAP
        return source * CHUNK + part * SLOTS + local * CAP + place

    across = stacked_from(lax.broadcasted_iota(jnp.int32, (1, GROUP_ROWS), 1))

    def sort_block(index, carry):
        at = pl.multiple_of(index * LANES, LANES)
        line = lax.broadcasted_iota(jnp.int32, (LANES, 1), 0) + at
        match = lax.broadcasted_iota(jnp.int32, (LANES, GROUP_ROWS), 1) == stacked_from(line)
        sort[pl.ds(at, LANES), :] = jnp.where(match, 1.0, 0.0).astype(bf16)
        unsort[pl.ds(at, LANES), :] = jnp.where(across == line, 1.0, 0.0).astype(bf16)
        return carry

    lax.fori_loop(0, GROUP_ROWS // LANES, sort_block, 0)


def send_kernel(rows, table, out):
    own = rows[...].reshape(ALL_ROWS, COLS)
    stacked = jnp.concatenate(
        [own[:, part * LANES : (part + 1) * LANES] for part in range(Q)], axis=0
    )
    out[...] = nn(table[...], stacked).astype(bf16)


def receive_kernel(step, arrived, table, out):
    for group in range(N_EP // GROUP):
        part = arrived[group * GROUP : (group + 1) * GROUP, step * CHUNK : (step + 1) * CHUNK, :]
        part = part.astype(f32).reshape(GROUP_ROWS, LANES).astype(bf16)
        sorted_rows = nn(table[...], part).astype(bf16)
        for piece in range(Q):
            for local in range(LOCAL):
                at = (piece * LOCAL + local) * BLOCK
                to = local * HALF + group * BLOCK
                out[to : to + BLOCK, piece * LANES : (piece + 1) * LANES] = sorted_rows[
                    at : at + BLOCK
                ]


def hidden_kernel(first, count, order, *refs):
    chunks = refs[:count]
    refs = refs[count:]
    before = None
    if first > 0:
        before, refs = refs[0], refs[1:]
    gate_all, up_all = refs[:2]
    outs = refs[2:-3]
    gate, up, sems = refs[-3:]

    def copies(index):
        at = pl.ds(pl.multiple_of(order[first + index] * COLS, COLS), COLS)
        return (
            pltpu.make_async_copy(gate_all.at[:, :, at], gate.at[index], sems.at[0, index]),
            pltpu.make_async_copy(up_all.at[:, :, at], up.at[index], sems.at[1, index]),
        )

    for index in range(count):
        for copy in copies(index):
            copy.start()
    if before is None:
        sums = [jnp.zeros((HALF, FR), f32) for _ in range(2 * LOCAL)]
    else:
        sums = [before[at] for at in range(2 * LOCAL)]
    for index in range(count):
        for copy in copies(index):
            copy.wait()
        for local in range(LOCAL):
            rows = chunks[index][local * HALF : (local + 1) * HALF, :]
            sums[2 * local] = sums[2 * local] + nt(rows, gate[index, local])
            sums[2 * local + 1] = sums[2 * local + 1] + nt(rows, up[index, local])
    if before is None:
        for at in range(2 * LOCAL):
            outs[0][at] = sums[at]
        return
    for local in range(LOCAL):
        value = (jax.nn.silu(sums[2 * local]) * sums[2 * local + 1]).astype(bf16)
        outs[0][:, local * FR : (local + 1) * FR] = value


def down_kernel(place, own, a, b, c, all_own, from_before, from_next, far_first, far_second, *refs):
    out, buffer, sems = refs
    mine = pl.ds(pl.multiple_of(place[0], COLS), COLS)
    inside = pl.ds(pl.multiple_of(place[1], COLS), COLS)
    copies = [
        pltpu.make_async_copy(all_own.at[:, :, mine], buffer.at[0], sems.at[0]),
        pltpu.make_async_copy(from_before.at[:, :, inside], buffer.at[1], sems.at[1]),
        pltpu.make_async_copy(from_next.at[:, :, inside], buffer.at[2], sems.at[2]),
        pltpu.make_async_copy(far_first.at[:, inside], buffer.at[3, 0], sems.at[3]),
        pltpu.make_async_copy(far_second.at[:, inside], buffer.at[3, 1], sems.at[4]),
    ]
    for copy in copies:
        copy.start()
    sums = [jnp.zeros((HALF, COLS), f32) for _ in range(LOCAL)]
    for index in range(4):
        copies[index].wait()
        if index == 3:
            copies[4].wait()
        units = (own, a, b, c)[index][...]
        for local in range(LOCAL):
            sums[local] = sums[local] + nn(
                units[:, local * FR : (local + 1) * FR], buffer[index, local]
            )
    for local in range(LOCAL):
        out[local * HALF : (local + 1) * HALF, :] = sums[local].astype(out.dtype)


def return_kernel(mine, other, table, out):
    total = (mine[...] + other[...].astype(f32)).astype(bf16)
    for group in range(N_EP // GROUP):
        pieces = []
        for piece in range(Q):
            for local in range(LOCAL):
                at = local * HALF + group * BLOCK
                pieces.append(total[at : at + BLOCK, piece * LANES : (piece + 1) * LANES])
        stacked = jnp.concatenate(pieces, axis=0)
        out[group * GROUP_ROWS : (group + 1) * GROUP_ROWS, :] = nn(table[...], stacked).astype(bf16)


def mix_kernel(first, second, high, low, out):
    total = jnp.zeros((Q * ALL_ROWS, LANES), f32)
    for step, back in enumerate((first, second)):
        rows = back[...]
        total = total + nn(high[step], rows) + nn(low[step], rows)
    total = total.astype(bf16)
    for part in range(Q):
        piece = total[part * ALL_ROWS : (part + 1) * ALL_ROWS]
        out[:, part * LANES : (part + 1) * LANES] = piece


def final_kernel(arrived, out):
    for part in range(N_REP):
        rows = arrived[part].astype(f32)
        for step in range(STEPS):
            out[step, :, part * COLS : (part + 1) * COLS] = rows[
                step * ROWS : (step + 1) * ROWS
            ].astype(bf16)


def rep_index(x, y):
    return (x % 4) * 2 + y % 2


NEXT = [(rep_index(x, y), rep_index(x + 1, y)) for x in range(4) for y in range(2)]
BEFORE = [(rep_index(x, y), rep_index(x - 1, y)) for x in range(4) for y in range(2)]
BESIDE = [(rep_index(x, y), rep_index(x, y + 1)) for x in range(4) for y in range(2)]


def go(value, pairs):
    return lax.ppermute(value, "rep", pairs)


def swap(value, axis):
    return lax.all_to_all(value, axis, split_axis=0, concat_axis=0, tiled=True)


def gathered(step, own):
    c = go(own, BESIDE)
    a = go(own, NEXT)
    b = go(own, BEFORE)
    if step == 0:
        f = go(a, NEXT)
    else:
        f = go(b, BEFORE)
    d = go(c, NEXT)
    e = go(c, BEFORE)
    k = go(f, BESIDE)
    return (own, a, b, c), (d, e, f, k)


def on_device(tokens, norm_gain, expert_ids, route_weights, w_gate, w_up, w_down):
    sds = jax.ShapeDtypeStruct
    me = lax.axis_index("rep")
    my_x = me // 2
    my_y = me % 2
    offset_x = jnp.array([0, 3, 1, 0, 3, 1, 2, 2], jnp.int32)
    offset_y = jnp.array([0, 0, 0, 1, 1, 1, 0, 1], jnp.int32)
    order = ((my_x + offset_x) % 4) * 2 + (my_y + offset_y) % 2
    here = jnp.arange(2, dtype=jnp.int32)
    place_mine = me * COLS * (1 - here) + my_y * COLS * here
    place_other = (me + 1 - 2 * my_y) * COLS * (1 - here) + (1 - my_y) * COLS * here

    normed = call(
        norm_kernel,
        sds((N_REP, STEPS * ROWS, COLS), bf16),
        (tokens.reshape(STEPS, ROWS, D), norm_gain.reshape(1, D)),
    )
    own = swap(normed, "rep")

    def slab(ahead, start, count):
        at = ((my_x + ahead) % 4) * 2 * COLS
        return lax.dynamic_slice(w_down, (start, 0, at), (count, FR, 2 * COLS))

    far = slab(2, 0, 1).reshape(FR, 2 * COLS), slab(2, 1, 1).reshape(FR, 2 * COLS)
    near = slab(1, 0, LOCAL), slab(3, 0, LOCAL)
    far, near, normed = lax.optimization_barrier((far, near, normed))
    far_first = go(far[0], NEXT)
    far_second = go(far[1], BEFORE)
    from_before = go(near[0], NEXT)
    from_next = go(near[1], BEFORE)
    far_first = go(far_first, NEXT)
    far_second = go(far_second, BEFORE)

    ids = expert_ids.reshape(STEPS, N_REP, ROWS, TOPK).swapaxes(0, 1).reshape(ALL_ROWS, TOPK)
    weights = route_weights.reshape(STEPS, N_REP, ROWS, TOPK).swapaxes(0, 1)
    send, keep_hi, keep_lo, sort, unsort = call(
        tables_kernel,
        [
            sds((STEPS * N_EP * CHUNK, Q * ALL_ROWS), bf16),
            sds((STEPS, Q * ALL_ROWS, N_EP * CHUNK), bf16),
            sds((STEPS, Q * ALL_ROWS, N_EP * CHUNK), bf16),
            sds((GROUP_ROWS, GROUP_ROWS), bf16),
            sds((GROUP_ROWS, GROUP_ROWS), bf16),
        ],
        (ids, weights.reshape(ALL_ROWS, TOPK)),
        limit=24,
    )

    outgoing = call(send_kernel, sds((STEPS * N_EP * CHUNK, LANES), bf16), (own, send), hbm=(1,))
    arrived = swap(outgoing.reshape(N_EP, STEPS * CHUNK, LANES), "ep")

    backs = []
    for step in range(STEPS):
        rows = call(
            lambda *refs, step=step: receive_kernel(step, *refs),
            sds((LOCAL * HALF, COLS), bf16),
            (arrived, sort),
            hbm=(1,),
        )
        sums = ()
        for first, parts in zip((0, 4), gathered(step, rows)):
            count = len(parts)
            operands = (order, *parts, *sums, w_gate, w_up)
            shape = sds((2 * LOCAL, HALF, FR), f32)
            if first > 0:
                shape = sds((HALF, LOCAL * FR), bf16)
            sums = [
                call(
                    lambda *refs, first=first, count=count: hidden_kernel(first, count, *refs),
                    shape,
                    operands,
                    memory={0: SMEM, len(operands) - 2: HBM, len(operands) - 1: HBM},
                    scratch=[
                        pltpu.VMEM((count, LOCAL, FR, COLS), bf16),
                        pltpu.VMEM((count, LOCAL, FR, COLS), bf16),
                        pltpu.SemaphoreType.DMA((2, count)),
                    ],
                    limit=16,
                )
            ]
        hidden = sums[0]
        a, b = go(hidden, NEXT), go(hidden, BEFORE)
        if step == 0:
            c = go(a, NEXT)
        else:
            c = go(b, BEFORE)

        def down(place, dtype):
            operands = (place, hidden, a, b, c, w_down)
            operands += (from_before, from_next, far_first, far_second)
            return call(
                down_kernel,
                sds((LOCAL * HALF, COLS), dtype),
                operands,
                memory={0: SMEM, **{at: HBM for at in range(5, 10)}},
                scratch=[
                    pltpu.VMEM((4, LOCAL, FR, COLS), bf16),
                    pltpu.SemaphoreType.DMA((5,)),
                ],
            )

        other = go(down(place_other, bf16), BESIDE)
        mine = down(place_mine, f32)
        results = call(
            return_kernel, sds((N_EP * CHUNK, LANES), bf16), (mine, other, unsort), hbm=(2,)
        )
        back = swap(results.reshape(N_EP, CHUNK, LANES), "ep")
        backs.append(back.reshape(N_EP * CHUNK, LANES))

    mixed = call(mix_kernel, sds((ALL_ROWS, COLS), bf16), (*backs, keep_hi, keep_lo), hbm=(2, 3))
    mixed = swap(mixed.reshape(N_REP, STEPS * ROWS, COLS), "rep")
    out = call(final_kernel, sds((STEPS, ROWS, D), bf16), (mixed,))
    return out[:, None, None]


def solution(mesh):
    return jax.shard_map(
        on_device,
        mesh=mesh,
        in_specs=(
            P(None, "ep", "rep", None, None),
            P(),
            P(None, "ep", None, None, None),
            P(None, "ep", None, None, None),
            P("ep", "rep", None),
            P("ep", "rep", None),
            P("ep", "rep", None),
        ),
        out_specs=P(None, "ep", "rep", None, None),
        check_vma=False,
    )
```

```python
import jax
import jax.numpy as jnp
from jax import lax
from jax.experimental import pallas as pl
from jax.experimental.pallas import tpu as pltpu
from jax.sharding import PartitionSpec as P

epsilon = 1e-06

STEPS = 2
N_REP = 8
N_EP = 32
ROWS = 4
D = 4096
FR = 192
LOCAL = 2
EXPERTS = 64
CAP = 5
TOPK = 8
COLS = D // N_REP
LANES = 128
Q = COLS // LANES
SLOTS = LOCAL * CAP
CHUNK = Q * SLOTS
ALL_ROWS = N_REP * STEPS * ROWS
HALF = N_EP * CAP
GROUP = 16
GROUP_ROWS = GROUP * CHUNK
BLOCK = GROUP * CAP


SMEM = pl.BlockSpec(memory_space=pltpu.SMEM)
HBM = pl.BlockSpec(memory_space=pltpu.HBM)
bf16 = jnp.bfloat16
f32 = jnp.float32


def nt(a, b):
    return lax.dot_general(a, b, (((1,), (1,)), ((), ())), preferred_element_type=f32)


def nn(a, b):
    return lax.dot_general(a, b, (((1,), (0,)), ((), ())), preferred_element_type=f32)


def small_div(value, by):
    return (value * ((1 << 20) // by + 1)) >> 20


def whole(shape):
    return pl.BlockSpec(
        shape, lambda index: (0,) * len(shape), pipeline_mode=pl.Buffered(buffer_count=1)
    )


def call(kernel, out_shapes, operands, memory=None, scratch=(), limit=12, hbm=()):
    memory = memory or {}
    many = isinstance(out_shapes, (list, tuple))
    out_specs = [whole(each.shape) for each in out_shapes] if many else whole(out_shapes.shape)
    operands = [
        pltpu.with_memory_space_constraint(each, pltpu.HBM)
        if at in hbm or memory.get(at) is HBM
        else each
        for at, each in enumerate(operands)
    ]
    return pl.pallas_call(
        kernel,
        out_shape=out_shapes,
        grid=(1,),
        in_specs=[memory.get(at, whole(each.shape)) for at, each in enumerate(operands)],
        out_specs=out_specs,
        scratch_shapes=list(scratch),
        compiler_params=pltpu.CompilerParams(vmem_limit_bytes=limit << 20),
    )(*operands)


def norm_kernel(tokens, gain, out):
    parts = []
    for step in range(STEPS):
        widened = tokens[step].astype(f32)
        mean = jnp.mean(widened * widened, axis=-1, keepdims=True)
        parts.append(widened * lax.rsqrt(mean + epsilon) * gain[...])
    both = jnp.concatenate(parts, axis=0).astype(bf16)
    for part in range(N_REP):
        out[part] = both[:, part * COLS : (part + 1) * COLS]


def positions(ids):
    chosen = ids[...]
    expert = lax.broadcasted_iota(jnp.int32, (ALL_ROWS, EXPERTS), 1)
    hits = [chosen[:, which : which + 1] == expert for which in range(TOPK)]
    member = sum(jnp.where(hit, 1.0, 0.0) for hit in hits)
    row = lax.broadcasted_iota(jnp.int32, (ALL_ROWS, ALL_ROWS), 0)
    other = lax.broadcasted_iota(jnp.int32, (ALL_ROWS, ALL_ROWS), 1)
    earlier = (other < row) & (((row >> 2) & 1) == ((other >> 2) & 1))
    position = nn(jnp.where(earlier, 1.0, 0.0).astype(bf16), member.astype(bf16))
    position = jnp.where(member > 0.5, position, 100.0).astype(bf16)
    return hits, jnp.concatenate([position] * Q, axis=0)


WIDE = 256


def split(line):
    target = small_div(line, 2 * CHUNK)
    rest = line - target * (2 * CHUNK)
    step = (rest >= CHUNK).astype(jnp.int32)
    rest = rest - step * CHUNK
    part = small_div(rest, SLOTS)
    slot = rest - part * SLOTS
    local = (slot >= CAP).astype(jnp.int32)
    return target * LOCAL + local, part * 2 + step, (slot - local * CAP).astype(f32)


def send_table_kernel(ids, send):
    _, position = positions(ids)
    column = lax.broadcasted_iota(jnp.int32, (1, Q * ALL_ROWS), 1)
    column = (column >> 6) * 2 + ((column >> 2) & 1)

    def block(index, carry):
        at = pl.multiple_of(index * WIDE, WIDE)
        bucket, piece, place = split(lax.broadcasted_iota(jnp.int32, (WIDE, 1), 0) + at)
        pick = lax.broadcasted_iota(jnp.int32, (WIDE, EXPERTS), 1) == bucket
        found = nt(jnp.where(pick, 1.0, 0.0).astype(bf16), position)
        right = (found == place) & (column == piece)
        send[pl.ds(at, WIDE), :] = jnp.where(right, 1.0, 0.0).astype(bf16)
        return carry

    lax.fori_loop(0, STEPS * N_EP * CHUNK // WIDE, block, 0)


def tables_kernel(ids, weights, keep_hi, keep_lo, sort, unsort):
    hits, position = positions(ids)
    shares = weights[...] / jnp.sum(weights[...], axis=-1, keepdims=True)
    share = sum(
        jnp.where(hit, shares[:, which : which + 1], 0.0) for which, hit in enumerate(hits)
    )
    share_hi = share.astype(bf16)
    share_lo = (share - share_hi.astype(f32)).astype(bf16)
    share_hi = jnp.concatenate([share_hi] * Q, axis=0)
    share_lo = jnp.concatenate([share_lo] * Q, axis=0)

    row = lax.broadcasted_iota(jnp.int32, (Q * ALL_ROWS, 1), 0)
    row = (row >> 6) * 2 + ((row >> 2) & 1)

    def keep_block(index, carry):
        at = pl.multiple_of(index * WIDE, WIDE)
        bucket, piece, place = split(lax.broadcasted_iota(jnp.int32, (1, WIDE), 1) + at)
        pick = lax.broadcasted_iota(jnp.int32, (EXPERTS, WIDE), 0) == bucket
        pick = jnp.where(pick, 1.0, 0.0).astype(bf16)
        right = (nn(position, pick) == place) & (row == piece)
        keep_hi[:, pl.ds(at, WIDE)] = jnp.where(right, nn(share_hi, pick), 0.0).astype(bf16)
        keep_lo[:, pl.ds(at, WIDE)] = jnp.where(right, nn(share_lo, pick), 0.0).astype(bf16)
        return carry

    lax.fori_loop(0, STEPS * N_EP * CHUNK // WIDE, keep_block, 0)

    def stacked_from(line):
        part = small_div(line, 2 * BLOCK)
        rest = line - part * (2 * BLOCK)
        local = (rest >= BLOCK).astype(jnp.int32)
        rest = rest - local * BLOCK
        source = small_div(rest, CAP)
        place = rest - source * CAP
        return source * CHUNK + part * SLOTS + local * CAP + place

    across = stacked_from(lax.broadcasted_iota(jnp.int32, (1, GROUP_ROWS), 1))

    def sort_block(index, carry):
        at = pl.multiple_of(index * LANES, LANES)
        line = lax.broadcasted_iota(jnp.int32, (LANES, 1), 0) + at
        match = lax.broadcasted_iota(jnp.int32, (LANES, GROUP_ROWS), 1) == stacked_from(line)
        sort[pl.ds(at, LANES), :] = jnp.where(match, 1.0, 0.0).astype(bf16)
        unsort[pl.ds(at, LANES), :] = jnp.where(across == line, 1.0, 0.0).astype(bf16)
        return carry

    lax.fori_loop(0, GROUP_ROWS // LANES, sort_block, 0)


def send_kernel(rows, table, out):
    own = rows[...].reshape(ALL_ROWS, COLS)
    stacked = jnp.concatenate(
        [own[:, part * LANES : (part + 1) * LANES] for part in range(Q)], axis=0
    )
    out[...] = nn(table[...], stacked).astype(bf16)


def cut_kernel(places, weights, far_first, far_second, near_next, near_before, sems):
    def source(which):
        return pl.ds(pl.multiple_of(places[which], 2 * COLS), 2 * COLS)

    copies = [
        pltpu.make_async_copy(weights.at[0, :, source(0)], far_first, sems.at[0]),
        pltpu.make_async_copy(weights.at[1, :, source(0)], far_second, sems.at[1]),
        pltpu.make_async_copy(weights.at[:, :, source(1)], near_next, sems.at[2]),
        pltpu.make_async_copy(weights.at[:, :, source(2)], near_before, sems.at[3]),
    ]
    for copy in copies:
        copy.start()
    for copy in copies:
        copy.wait()


def receive_kernel(arrived, table, *outs):
    for step in range(STEPS):
        for group in range(N_EP // GROUP):
            part = arrived[
                group * GROUP : (group + 1) * GROUP, step * CHUNK : (step + 1) * CHUNK, :
            ]
            part = part.astype(f32).reshape(GROUP_ROWS, LANES).astype(bf16)
            sorted_rows = nn(table[...], part).astype(bf16)
            for piece in range(Q):
                for local in range(LOCAL):
                    at = (piece * LOCAL + local) * BLOCK
                    to = local * HALF + group * BLOCK
                    for out, shift in ((outs[step], 0), (outs[2], step * LOCAL * HALF)):
                        out[
                            shift + to : shift + to + BLOCK, piece * LANES : (piece + 1) * LANES
                        ] = sorted_rows[at : at + BLOCK]


def rows_of(refs, local):
    both = []
    for step in range(STEPS):
        if len(refs) == STEPS:
            both.append(refs[step][local * HALF : (local + 1) * HALF, :])
        else:
            at = (step * LOCAL + local) * HALF
            both.append(refs[0][at : at + HALF, :])
    return jnp.concatenate(both, axis=0)


def hidden_kernel(first, sizes, order, *refs):
    count = len(sizes)
    chunks = []
    for size in sizes:
        chunks.append(refs[:size])
        refs = refs[size:]
    before = None
    if first > 0:
        before, refs = refs[0], refs[1:]
    gate_all, up_all = refs[:2]
    outs = refs[2:-3]
    gate, up, sems = refs[-3:]

    def copies(index):
        at = pl.ds(pl.multiple_of(order[first + index] * COLS, COLS), COLS)
        return (
            pltpu.make_async_copy(gate_all.at[:, :, at], gate.at[index], sems.at[0, index]),
            pltpu.make_async_copy(up_all.at[:, :, at], up.at[index], sems.at[1, index]),
        )

    for index in range(count):
        for copy in copies(index):
            copy.start()
    sums = [None] * (2 * LOCAL)
    if before is not None:
        sums = [before[at] for at in range(2 * LOCAL)]
    for index in range(count):
        for copy in copies(index):
            copy.wait()
        for local in range(LOCAL):
            rows = rows_of(chunks[index], local)
            for which, weights in enumerate((gate, up)):
                at = 2 * local + which
                product = nt(rows, weights[index, local])
                sums[at] = product if sums[at] is None else sums[at] + product
    if before is None:
        for at in range(2 * LOCAL):
            outs[0][at] = sums[at]
        return
    for local in range(LOCAL):
        value = (jax.nn.silu(sums[2 * local]) * sums[2 * local + 1]).astype(bf16)
        for step in range(STEPS):
            outs[step][:, local * FR : (local + 1) * FR] = value[step * HALF : (step + 1) * HALF]


def down_kernel(place, *refs):
    units = [refs[2 * index : 2 * index + 2] for index in range(4)]
    all_own, from_before, from_next, far_first, far_second, out, buffer, sems = refs[8:]
    mine = pl.ds(pl.multiple_of(place[0], COLS), COLS)
    inside = pl.ds(pl.multiple_of(place[1], COLS), COLS)
    copies = [
        pltpu.make_async_copy(all_own.at[:, :, mine], buffer.at[0], sems.at[0]),
        pltpu.make_async_copy(from_before.at[:, :, inside], buffer.at[1], sems.at[1]),
        pltpu.make_async_copy(from_next.at[:, :, inside], buffer.at[2], sems.at[2]),
        pltpu.make_async_copy(far_first.at[:, inside], buffer.at[3, 0], sems.at[3]),
        pltpu.make_async_copy(far_second.at[:, inside], buffer.at[3, 1], sems.at[4]),
    ]
    for copy in copies:
        copy.start()
    sums = [None] * LOCAL
    for index in range(4):
        copies[index].wait()
        if index == 3:
            copies[4].wait()
        both = jnp.concatenate([units[index][step][...] for step in range(STEPS)], axis=0)
        for local in range(LOCAL):
            product = nn(both[:, local * FR : (local + 1) * FR], buffer[index, local])
            sums[local] = product if sums[local] is None else sums[local] + product
    for local in range(LOCAL):
        for step in range(STEPS):
            at = (step * LOCAL + local) * HALF
            out[at : at + HALF, :] = sums[local][step * HALF : (step + 1) * HALF].astype(out.dtype)


def return_kernel(mine, other, table, out):
    for step in range(STEPS):
        for group in range(N_EP // GROUP):
            pieces = []
            for piece in range(Q):
                for local in range(LOCAL):
                    at = (step * LOCAL + local) * HALF + group * BLOCK
                    span = (slice(at, at + BLOCK), slice(piece * LANES, (piece + 1) * LANES))
                    pieces.append((mine[span] + other[span].astype(f32)).astype(bf16))
            stacked = jnp.concatenate(pieces, axis=0)
            result = nn(table[...], stacked).reshape(GROUP, CHUNK, LANES).astype(bf16)
            out[group * GROUP : (group + 1) * GROUP, step * CHUNK : (step + 1) * CHUNK, :] = result


def mix_kernel(back, high, low, out):
    rows = back[...]
    total = (nn(high[...], rows) + nn(low[...], rows)).astype(bf16)
    for part in range(Q):
        piece = total[part * ALL_ROWS : (part + 1) * ALL_ROWS]
        out[:, part * LANES : (part + 1) * LANES] = piece


def final_kernel(arrived, out):
    for part in range(N_REP):
        rows = arrived[part].astype(f32)
        for step in range(STEPS):
            out[step, :, part * COLS : (part + 1) * COLS] = rows[
                step * ROWS : (step + 1) * ROWS
            ].astype(bf16)


def rep_index(x, y):
    return (x % 4) * 2 + y % 2


NEXT = [(rep_index(x, y), rep_index(x + 1, y)) for x in range(4) for y in range(2)]
BEFORE = [(rep_index(x, y), rep_index(x - 1, y)) for x in range(4) for y in range(2)]
BESIDE = [(rep_index(x, y), rep_index(x, y + 1)) for x in range(4) for y in range(2)]


def go(value, pairs):
    return lax.ppermute(value, "rep", pairs)


def swap(value, axis):
    return lax.all_to_all(value, axis, split_axis=0, concat_axis=0, tiled=True)


def gathered(own0, own1, both):
    c = go(both, BESIDE)
    a0 = go(own0, NEXT)
    b1 = go(own1, BEFORE)
    a1 = go(own1, NEXT)
    b0 = go(own0, BEFORE)
    f0 = go(a0, NEXT)
    f1 = go(b1, BEFORE)
    d = go(c, NEXT)
    e = go(c, BEFORE)
    k0 = go(f0, BESIDE)
    k1 = go(f1, BESIDE)
    return ((own0, own1), (a0, a1), (b0, b1), (c,)), ((d,), (e,), (f0, f1), (k0, k1))


def on_device(tokens, norm_gain, expert_ids, route_weights, w_gate, w_up, w_down):
    sds = jax.ShapeDtypeStruct
    me = lax.axis_index("rep")
    my_x = me // 2
    my_y = me % 2
    offset_x = jnp.array([0, 3, 1, 0, 3, 1, 2, 2], jnp.int32)
    offset_y = jnp.array([0, 0, 0, 1, 1, 1, 0, 1], jnp.int32)
    order = ((my_x + offset_x) % 4) * 2 + (my_y + offset_y) % 2
    here = jnp.arange(2, dtype=jnp.int32)
    place_mine = me * COLS * (1 - here) + my_y * COLS * here
    place_other = (me + 1 - 2 * my_y) * COLS * (1 - here) + (1 - my_y) * COLS * here

    normed = call(
        norm_kernel,
        sds((N_REP, STEPS * ROWS, COLS), bf16),
        (tokens.reshape(STEPS, ROWS, D), norm_gain.reshape(1, D)),
        hbm=(0, 1),
    )
    own = swap(normed, "rep")

    steps_ahead = jnp.array([2, 1, 3], jnp.int32)
    places = ((my_x + steps_ahead) % 4) * (2 * COLS)
    far_shape, near_shape = sds((FR, 2 * COLS), bf16), sds((LOCAL, FR, 2 * COLS), bf16)
    far_first, far_second, near_next, near_before = call(
        cut_kernel,
        [far_shape, far_shape, near_shape, near_shape],
        (places, w_down),
        memory={0: SMEM, 1: HBM},
        scratch=[pltpu.SemaphoreType.DMA((4,))],
    )
    far_first = go(far_first, NEXT)
    far_second = go(far_second, BEFORE)
    from_before = go(near_next, NEXT)
    from_next = go(near_before, BEFORE)
    far_first = go(far_first, NEXT)
    far_second = go(far_second, BEFORE)

    ids = expert_ids.reshape(STEPS, N_REP, ROWS, TOPK).swapaxes(0, 1).reshape(ALL_ROWS, TOPK)
    weights = route_weights.reshape(STEPS, N_REP, ROWS, TOPK).swapaxes(0, 1)
    weights = weights.reshape(ALL_ROWS, TOPK)
    slots = STEPS * N_EP * CHUNK
    send = call(send_table_kernel, sds((slots, Q * ALL_ROWS), bf16), (ids,))
    keep_hi, keep_lo, sort, unsort = call(
        tables_kernel,
        [
            sds((Q * ALL_ROWS, slots), bf16),
            sds((Q * ALL_ROWS, slots), bf16),
            sds((GROUP_ROWS, GROUP_ROWS), bf16),
            sds((GROUP_ROWS, GROUP_ROWS), bf16),
        ],
        (ids, weights),
    )

    outgoing = call(send_kernel, sds((slots, LANES), bf16), (own, send))
    arrived = swap(outgoing.reshape(N_EP, STEPS * CHUNK, LANES), "ep")

    one, two = sds((LOCAL * HALF, COLS), bf16), sds((STEPS * LOCAL * HALF, COLS), bf16)
    rows = call(receive_kernel, [one, one, two], (arrived, sort))
    sums = ()
    for first, parts in zip((0, 4), gathered(*rows)):
        sizes = tuple(len(part) for part in parts)
        chunks = tuple(each for part in parts for each in part)
        operands = (order, *chunks, *sums, w_gate, w_up)
        shapes = [sds((2 * LOCAL, STEPS * HALF, FR), f32)]
        if first > 0:
            shapes = [sds((HALF, LOCAL * FR), bf16)] * STEPS
        sums = call(
            lambda *refs, first=first, sizes=sizes: hidden_kernel(first, sizes, *refs),
            shapes,
            operands,
            memory={0: SMEM, len(operands) - 2: HBM, len(operands) - 1: HBM},
            scratch=[
                pltpu.VMEM((4, LOCAL, FR, COLS), bf16),
                pltpu.VMEM((4, LOCAL, FR, COLS), bf16),
                pltpu.SemaphoreType.DMA((2, 4)),
            ],
            limit=20,
        )
    hidden0, hidden1 = sums
    a0, b1 = go(hidden0, NEXT), go(hidden1, BEFORE)
    a1, b0 = go(hidden1, NEXT), go(hidden0, BEFORE)
    c0, c1 = go(a0, NEXT), go(b1, BEFORE)
    units = (hidden0, hidden1, a0, a1, b0, b1, c0, c1)

    def down(place, dtype):
        operands = (place, *units, w_down, from_before, from_next, far_first, far_second)
        return call(
            down_kernel,
            sds((STEPS * LOCAL * HALF, COLS), dtype),
            operands,
            memory={0: SMEM, **{at: HBM for at in range(9, 14)}},
            scratch=[
                pltpu.VMEM((4, LOCAL, FR, COLS), bf16),
                pltpu.SemaphoreType.DMA((5,)),
            ],
        )

    other = go(down(place_other, bf16), BESIDE)
    mine = down(place_mine, f32)
    back = call(return_kernel, sds((N_EP, STEPS * CHUNK, LANES), bf16), (mine, other, unsort))
    back = swap(back, "ep").reshape(slots, LANES)
    mixed = call(mix_kernel, sds((ALL_ROWS, COLS), bf16), (back, keep_hi, keep_lo), hbm=(1, 2))
    mixed = swap(mixed.reshape(N_REP, STEPS * ROWS, COLS), "rep")
    out = call(final_kernel, sds((STEPS, ROWS, D), bf16), (mixed,))
    return out[:, None, None]


def solution(mesh):
    return jax.shard_map(
        on_device,
        mesh=mesh,
        in_specs=(
            P(None, "ep", "rep", None, None),
            P(),
            P(None, "ep", None, None, None),
            P(None, "ep", None, None, None),
            P("ep", "rep", None),
            P("ep", "rep", None),
            P("ep", "rep", None),
        ),
        out_specs=P(None, "ep", "rep", None, None),
        check_vma=False,
    )
```

```python
from functools import partial

import jax
import jax.numpy as jnp
from jax import lax
from jax.experimental import pallas as pl
from jax.experimental.pallas import tpu as pltpu
from jax.sharding import PartitionSpec as P

epsilon = 1e-06

STEPS = 2
N_REP = 8
N_EP = 32
ROWS = 4
D = 4096
FR = 192
LOCAL = 2
EXPERTS = 64
CAP = 5
TOPK = 8
COLS = D // N_REP
LANES = 128
Q = COLS // LANES
SLOTS = LOCAL * CAP
CHUNK = Q * SLOTS
ALL_ROWS = N_REP * STEPS * ROWS
HALF = N_EP * CAP
GROUP = 16
GROUP_ROWS = GROUP * CHUNK
BLOCK = GROUP * CAP


HBM = pl.BlockSpec(memory_space=pltpu.HBM)
VMEM = pl.BlockSpec(memory_space=pltpu.VMEM)
bf16 = jnp.bfloat16
f32 = jnp.float32


def nt(a, b):
    return lax.dot_general(a, b, (((1,), (1,)), ((), ())), preferred_element_type=f32)


def nn(a, b):
    return lax.dot_general(a, b, (((1,), (0,)), ((), ())), preferred_element_type=f32)


def small_div(value, by):
    return (value * ((1 << 20) // by + 1)) >> 20


def whole(shape):
    return pl.BlockSpec(
        shape, lambda index: (0,) * len(shape), pipeline_mode=pl.Buffered(buffer_count=1)
    )


def call(kernel, out_shapes, operands, memory=None, scratch=(), limit=12, hbm=(), out=None):
    memory = memory or {}
    many = isinstance(out_shapes, (list, tuple))
    out_specs = [whole(each.shape) for each in out_shapes] if many else whole(out_shapes.shape)
    if out is not None:
        out_specs = [out] * len(out_shapes)
    operands = [
        pltpu.with_memory_space_constraint(each, pltpu.HBM)
        if at in hbm or memory.get(at) is HBM
        else each
        for at, each in enumerate(operands)
    ]
    return pl.pallas_call(
        kernel,
        out_shape=out_shapes,
        grid=(1,),
        in_specs=[memory.get(at, whole(each.shape)) for at, each in enumerate(operands)],
        out_specs=out_specs,
        scratch_shapes=list(scratch),
        compiler_params=pltpu.CompilerParams(vmem_limit_bytes=limit << 20),
    )(*operands)


def norm_kernel(tokens, gain, out):
    parts = []
    for step in range(STEPS):
        widened = tokens[step].astype(f32)
        mean = jnp.mean(widened * widened, axis=-1, keepdims=True)
        parts.append(widened * lax.rsqrt(mean + epsilon) * gain[...])
    both = jnp.concatenate(parts, axis=0).astype(bf16)
    for part in range(N_REP):
        out[part] = both[:, part * COLS : (part + 1) * COLS]


def positions(ids):
    chosen = ids[...]
    expert = lax.broadcasted_iota(jnp.int32, (ALL_ROWS, EXPERTS), 1)
    hits = [chosen[:, which : which + 1] == expert for which in range(TOPK)]
    member = sum(jnp.where(hit, 1.0, 0.0) for hit in hits)
    row = lax.broadcasted_iota(jnp.int32, (ALL_ROWS, ALL_ROWS), 0)
    other = lax.broadcasted_iota(jnp.int32, (ALL_ROWS, ALL_ROWS), 1)
    earlier = (other < row) & (((row >> 2) & 1) == ((other >> 2) & 1))
    position = nn(jnp.where(earlier, 1.0, 0.0).astype(bf16), member.astype(bf16))
    position = jnp.where(member > 0.5, position, 100.0).astype(bf16)
    return hits, jnp.concatenate([position] * Q, axis=0)


WIDE = 256


def split(line):
    target = small_div(line, 2 * CHUNK)
    rest = line - target * (2 * CHUNK)
    step = (rest >= CHUNK).astype(jnp.int32)
    rest = rest - step * CHUNK
    part = small_div(rest, SLOTS)
    slot = rest - part * SLOTS
    local = (slot >= CAP).astype(jnp.int32)
    return target * LOCAL + local, part * 2 + step, (slot - local * CAP).astype(f32)


def send_table_kernel(ids, send):
    _, position = positions(ids)
    column = lax.broadcasted_iota(jnp.int32, (1, Q * ALL_ROWS), 1)
    column = (column >> 6) * 2 + ((column >> 2) & 1)

    def block(index, carry):
        at = pl.multiple_of(index * WIDE, WIDE)
        bucket, piece, place = split(lax.broadcasted_iota(jnp.int32, (WIDE, 1), 0) + at)
        pick = lax.broadcasted_iota(jnp.int32, (WIDE, EXPERTS), 1) == bucket
        found = nt(jnp.where(pick, 1.0, 0.0).astype(bf16), position)
        right = (found == place) & (column == piece)
        send[pl.ds(at, WIDE), :] = jnp.where(right, 1.0, 0.0).astype(bf16)
        return carry

    lax.fori_loop(0, STEPS * N_EP * CHUNK // WIDE, block, 0, unroll=5)


def tables_kernel(ids, weights, keep, sort, unsort):
    hits, position = positions(ids)
    shares = weights[...] / jnp.sum(weights[...], axis=-1, keepdims=True)
    share = sum(
        jnp.where(hit, shares[:, which : which + 1], 0.0) for which, hit in enumerate(hits)
    )
    share = jnp.concatenate([share.astype(bf16)] * Q, axis=0)
    row = lax.broadcasted_iota(jnp.int32, (Q * ALL_ROWS, 1), 0)
    row = (row >> 6) * 2 + ((row >> 2) & 1)

    def keep_block(index, carry):
        at = pl.multiple_of(index * WIDE, WIDE)
        bucket, piece, place = split(lax.broadcasted_iota(jnp.int32, (1, WIDE), 1) + at)
        pick = lax.broadcasted_iota(jnp.int32, (EXPERTS, WIDE), 0) == bucket
        pick = jnp.where(pick, 1.0, 0.0).astype(bf16)
        right = (nn(position, pick) == place) & (row == piece)
        keep[:, pl.ds(at, WIDE)] = jnp.where(right, nn(share, pick), 0.0).astype(bf16)
        return carry

    lax.fori_loop(0, STEPS * N_EP * CHUNK // WIDE, keep_block, 0)

    def stacked_from(line):
        part = small_div(line, 2 * BLOCK)
        rest = line - part * (2 * BLOCK)
        local = (rest >= BLOCK).astype(jnp.int32)
        rest = rest - local * BLOCK
        source = small_div(rest, CAP)
        place = rest - source * CAP
        return source * CHUNK + part * SLOTS + local * CAP + place

    across = stacked_from(lax.broadcasted_iota(jnp.int32, (1, GROUP_ROWS), 1))

    def sort_block(index, carry):
        at = pl.multiple_of(index * LANES, LANES)
        line = lax.broadcasted_iota(jnp.int32, (LANES, 1), 0) + at
        match = lax.broadcasted_iota(jnp.int32, (LANES, GROUP_ROWS), 1) == stacked_from(line)
        sort[pl.ds(at, LANES), :] = jnp.where(match, 1.0, 0.0).astype(bf16)
        unsort[pl.ds(at, LANES), :] = jnp.where(across == line, 1.0, 0.0).astype(bf16)
        return carry

    lax.fori_loop(0, GROUP_ROWS // LANES, sort_block, 0)


def send_kernel(rows, table, out):
    own = rows[...].reshape(ALL_ROWS, COLS)
    stacked = jnp.concatenate(
        [own[:, part * LANES : (part + 1) * LANES] for part in range(Q)], axis=0
    )
    out[...] = nn(table[...], stacked).astype(bf16)


def my_place():
    me = lax.axis_index("rep")
    return me >> 1, me & 1


OFFSETS = ((0, 0), (3, 0), (1, 0), (0, 1), (3, 1), (1, 1), (2, 0), (2, 1))


def slab(ahead):
    x, _ = my_place()
    return pl.ds(pl.multiple_of(((x + ahead) & 3) * (2 * COLS), 2 * COLS), 2 * COLS)


def run_all(copies):
    for copy in copies:
        copy.start()
    for copy in copies:
        copy.wait()


def near_kernel(weights, near_next, near_before, sems):
    run_all(
        [
            pltpu.make_async_copy(weights.at[:, :, slab(1)], near_next, sems.at[0]),
            pltpu.make_async_copy(weights.at[:, :, slab(3)], near_before, sems.at[1]),
        ]
    )


def far_kernel(weights, far_first, far_second, sems):
    run_all(
        [
            pltpu.make_async_copy(weights.at[0, :, slab(2)], far_first, sems.at[0]),
            pltpu.make_async_copy(weights.at[1, :, slab(2)], far_second, sems.at[1]),
        ]
    )


def receive_kernel(arrived, table, *outs):
    for step in range(STEPS):
        for group in range(N_EP // GROUP):
            part = arrived[
                group * GROUP : (group + 1) * GROUP, step * CHUNK : (step + 1) * CHUNK, :
            ]
            part = part.astype(f32).reshape(GROUP_ROWS, LANES).astype(bf16)
            sorted_rows = nn(table[...], part).astype(bf16)
            for piece in range(Q):
                for local in range(LOCAL):
                    at = (piece * LOCAL + local) * BLOCK
                    to = local * HALF + group * BLOCK
                    for out, shift in ((outs[step], 0), (outs[2], step * LOCAL * HALF)):
                        out[
                            shift + to : shift + to + BLOCK, piece * LANES : (piece + 1) * LANES
                        ] = sorted_rows[at : at + BLOCK]


def rows_of(refs, local):
    both = []
    for step in range(STEPS):
        if len(refs) == STEPS:
            both.append(refs[step][local * HALF : (local + 1) * HALF, :])
        else:
            at = (step * LOCAL + local) * HALF
            both.append(refs[0][at : at + HALF, :])
    return jnp.concatenate(both, axis=0)


def hidden_kernel(which_chunks, last, sizes, *refs):
    count = len(sizes)
    chunks = []
    for size in sizes:
        chunks.append(refs[:size])
        refs = refs[size:]
    before = None
    if which_chunks[0] > 0:
        before, refs = refs[0], refs[1:]
    gate_all, up_all = refs[:2]
    outs = refs[2:-3]
    gate, up, sems = refs[-3:]

    def copies(index):
        ahead, aside = OFFSETS[which_chunks[index]]
        x, y = my_place()
        chunk = ((x + ahead) & 3) * 2 + (y ^ aside)
        at = pl.ds(pl.multiple_of(chunk * COLS, COLS), COLS)
        return (
            pltpu.make_async_copy(gate_all.at[:, :, at], gate.at[index], sems.at[0, index]),
            pltpu.make_async_copy(up_all.at[:, :, at], up.at[index], sems.at[1, index]),
        )

    for index in range(count):
        for copy in copies(index):
            copy.start()
    sums = [None] * (2 * LOCAL)
    if before is not None:
        sums = [before[at] for at in range(2 * LOCAL)]
    for index in range(count):
        for copy in copies(index):
            copy.wait()
        for local in range(LOCAL):
            rows = rows_of(chunks[index], local)
            for which, weights in enumerate((gate, up)):
                at = 2 * local + which
                product = nt(rows, weights[index, local])
                sums[at] = product if sums[at] is None else sums[at] + product
    if not last:
        for at in range(2 * LOCAL):
            outs[0][at] = sums[at]
        return
    for local in range(LOCAL):
        value = (jax.nn.silu(sums[2 * local]) * sums[2 * local + 1]).astype(bf16)
        for step in range(STEPS):
            outs[step][:, local * FR : (local + 1) * FR] = value[step * HALF : (step + 1) * HALF]


def down_kernel(aside, *refs):
    units = [refs[2 * index : 2 * index + 2] for index in range(4)]
    all_own, from_before, from_next, far_first, far_second, out, buffer, sems = refs[8:]
    x, y = my_place()
    mine = pl.ds(pl.multiple_of((x * 2 + (y ^ aside)) * COLS, COLS), COLS)
    inside = pl.ds(pl.multiple_of((y ^ aside) * COLS, COLS), COLS)
    copies = [
        pltpu.make_async_copy(all_own.at[:, :, mine], buffer.at[0], sems.at[0]),
        pltpu.make_async_copy(from_before.at[:, :, inside], buffer.at[1], sems.at[1]),
        pltpu.make_async_copy(from_next.at[:, :, inside], buffer.at[2], sems.at[2]),
        pltpu.make_async_copy(far_first.at[:, inside], buffer.at[3, 0], sems.at[3]),
        pltpu.make_async_copy(far_second.at[:, inside], buffer.at[3, 1], sems.at[4]),
    ]
    for copy in copies:
        copy.start()
    sums = [None] * LOCAL
    for index in range(4):
        copies[index].wait()
        if index == 3:
            copies[4].wait()
        both = jnp.concatenate([units[index][step][...] for step in range(STEPS)], axis=0)
        for local in range(LOCAL):
            product = nn(both[:, local * FR : (local + 1) * FR], buffer[index, local])
            sums[local] = product if sums[local] is None else sums[local] + product
    for local in range(LOCAL):
        for step in range(STEPS):
            at = (step * LOCAL + local) * HALF
            out[at : at + HALF, :] = sums[local][step * HALF : (step + 1) * HALF].astype(out.dtype)


def return_kernel(mine, other, table, out):
    for step in range(STEPS):
        for group in range(N_EP // GROUP):
            pieces = []
            for piece in range(Q):
                for local in range(LOCAL):
                    at = (step * LOCAL + local) * HALF + group * BLOCK
                    span = (slice(at, at + BLOCK), slice(piece * LANES, (piece + 1) * LANES))
                    pieces.append((mine[span] + other[span].astype(f32)).astype(bf16))
            stacked = jnp.concatenate(pieces, axis=0)
            result = nn(table[...], stacked).reshape(GROUP, CHUNK, LANES).astype(bf16)
            out[group * GROUP : (group + 1) * GROUP, step * CHUNK : (step + 1) * CHUNK, :] = result


def mix_kernel(back, keep, out):
    total = nn(keep[...], back[...]).astype(bf16)
    for part in range(Q):
        piece = total[part * ALL_ROWS : (part + 1) * ALL_ROWS]
        out[:, part * LANES : (part + 1) * LANES] = piece


def final_kernel(arrived, out):
    for part in range(N_REP):
        rows = arrived[part].astype(f32)
        for step in range(STEPS):
            out[step, :, part * COLS : (part + 1) * COLS] = rows[
                step * ROWS : (step + 1) * ROWS
            ].astype(bf16)


def rep_index(x, y):
    return (x % 4) * 2 + y % 2


NEXT = [(rep_index(x, y), rep_index(x + 1, y)) for x in range(4) for y in range(2)]
BEFORE = [(rep_index(x, y), rep_index(x - 1, y)) for x in range(4) for y in range(2)]
BESIDE = [(rep_index(x, y), rep_index(x, y + 1)) for x in range(4) for y in range(2)]


def go(value, pairs):
    return lax.ppermute(value, "rep", pairs)


def swap(value, axis):
    return lax.all_to_all(value, axis, split_axis=0, concat_axis=0, tiled=True)


def gathered(own0, own1, both):
    c = go(both, BESIDE)
    a0 = go(own0, NEXT)
    b1 = go(own1, BEFORE)
    a1 = go(own1, NEXT)
    b0 = go(own0, BEFORE)
    f0 = go(a0, NEXT)
    f1 = go(b1, BEFORE)
    d = go(c, NEXT)
    e = go(c, BEFORE)
    k0 = go(f0, BESIDE)
    k1 = go(f1, BESIDE)
    return ((own0, own1), (a0, a1), (b0, b1), (c,)), ((d,), (e,), (f0, f1), (k0, k1))


def on_device(tokens, norm_gain, expert_ids, route_weights, w_gate, w_up, w_down):
    sds = jax.ShapeDtypeStruct
    normed = call(
        norm_kernel,
        sds((N_REP, STEPS * ROWS, COLS), bf16),
        (tokens.reshape(STEPS, ROWS, D), norm_gain.reshape(1, D)),
        hbm=(0, 1),
    )
    own = swap(normed, "rep")

    far_shape, near_shape = sds((FR, 2 * COLS), bf16), sds((LOCAL, FR, 2 * COLS), bf16)

    def cut(kernel, shape):
        scratch = [pltpu.SemaphoreType.DMA((2,))]
        return call(kernel, [shape] * 2, (w_down,), memory={0: HBM}, scratch=scratch, out=VMEM)

    near_next, near_before = cut(near_kernel, near_shape)
    far_first, far_second = cut(far_kernel, far_shape)
    from_before = go(near_next, NEXT)
    from_next = go(near_before, BEFORE)
    far_first = go(far_first, NEXT)
    far_second = go(far_second, BEFORE)
    far_first = go(far_first, NEXT)
    far_second = go(far_second, BEFORE)

    ids = expert_ids.reshape(STEPS, N_REP, ROWS, TOPK).swapaxes(0, 1).reshape(ALL_ROWS, TOPK)
    weights = route_weights.reshape(STEPS, N_REP, ROWS, TOPK).swapaxes(0, 1)
    weights = weights.reshape(ALL_ROWS, TOPK)
    slots = STEPS * N_EP * CHUNK
    send = call(send_table_kernel, sds((slots, Q * ALL_ROWS), bf16), (ids,))
    keep, sort, unsort = call(
        tables_kernel,
        [
            sds((Q * ALL_ROWS, slots), bf16),
            sds((GROUP_ROWS, GROUP_ROWS), bf16),
            sds((GROUP_ROWS, GROUP_ROWS), bf16),
        ],
        (ids, weights),
    )

    outgoing = call(send_kernel, sds((slots, LANES), bf16), (own, send))
    arrived = swap(outgoing.reshape(N_EP, STEPS * CHUNK, LANES), "ep")

    one, two = sds((LOCAL * HALF, COLS), bf16), sds((STEPS * LOCAL * HALF, COLS), bf16)
    rows = call(receive_kernel, [one, one, two], (arrived, sort))
    sums = ()
    early, late = gathered(*rows)
    every = (*early, *late)
    for name, which in (("early", (0, 1, 2, 3)), ("middle", (6,)), ("late", (4, 5, 7))):
        parts = [every[index] for index in which]
        sizes = tuple(len(part) for part in parts)
        count = len(sizes)
        last = name == "late"
        chunks = tuple(each for part in parts for each in part)
        operands = (*chunks, *sums, w_gate, w_up)
        shapes = [sds((2 * LOCAL, STEPS * HALF, FR), f32)]
        if last:
            shapes = [sds((HALF, LOCAL * FR), bf16)] * STEPS
        sums = call(
            partial(hidden_kernel, which, last, sizes),
            shapes,
            operands,
            memory={len(operands) - 2: HBM, len(operands) - 1: HBM},
            scratch=[
                pltpu.VMEM((count, LOCAL, FR, COLS), bf16),
                pltpu.VMEM((count, LOCAL, FR, COLS), bf16),
                pltpu.SemaphoreType.DMA((2, count)),
            ],
            limit=20,
        )
    hidden0, hidden1 = sums
    a0, b1 = go(hidden0, NEXT), go(hidden1, BEFORE)
    a1, b0 = go(hidden1, NEXT), go(hidden0, BEFORE)
    c0, c1 = go(a0, NEXT), go(b1, BEFORE)
    units = (hidden0, hidden1, a0, a1, b0, b1, c0, c1)

    def down(aside, dtype):
        operands = (*units, w_down, from_before, from_next, far_first, far_second)
        return call(
            partial(down_kernel, aside),
            sds((STEPS * LOCAL * HALF, COLS), dtype),
            operands,
            memory={at: HBM for at in range(8, 13)},
            scratch=[
                pltpu.VMEM((4, LOCAL, FR, COLS), bf16),
                pltpu.SemaphoreType.DMA((5,)),
            ],
        )

    other = go(down(1, bf16), BESIDE)
    mine = down(0, f32)
    back = call(return_kernel, sds((N_EP, STEPS * CHUNK, LANES), bf16), (mine, other, unsort))
    back = swap(back, "ep").reshape(slots, LANES)
    mixed = call(mix_kernel, sds((ALL_ROWS, COLS), bf16), (back, keep), hbm=(1,))
    mixed = swap(mixed.reshape(N_REP, STEPS * ROWS, COLS), "rep")
    out = call(final_kernel, sds((STEPS, ROWS, D), bf16), (mixed,))
    return out[:, None, None]


def solution(mesh):
    return jax.shard_map(
        on_device,
        mesh=mesh,
        in_specs=(
            P(None, "ep", "rep", None, None),
            P(),
            P(None, "ep", None, None, None),
            P(None, "ep", None, None, None),
            P("ep", "rep", None),
            P("ep", "rep", None),
            P("ep", "rep", None),
        ),
        out_specs=P(None, "ep", "rep", None, None),
        check_vma=False,
    )
```

```python
from functools import partial

import jax
import jax.numpy as jnp
from jax import lax
from jax.experimental import pallas as pl
from jax.experimental.pallas import tpu as pltpu
from jax.sharding import PartitionSpec as P

epsilon = 1e-06

STEPS = 2
N_REP = 8
N_EP = 32
ROWS = 4
D = 4096
FR = 192
LOCAL = 2
EXPERTS = 64
CAP = 5
TOPK = 8
COLS = D // N_REP
LANES = 128
Q = COLS // LANES
SLOTS = LOCAL * CAP
CHUNK = Q * SLOTS
ALL_ROWS = N_REP * STEPS * ROWS
HALF = N_EP * CAP
GROUP = 16
GROUP_ROWS = GROUP * CHUNK
BLOCK = GROUP * CAP


HBM = pl.BlockSpec(memory_space=pltpu.HBM)
VMEM = pl.BlockSpec(memory_space=pltpu.VMEM)
bf16 = jnp.bfloat16
f32 = jnp.float32


def nt(a, b):
    return lax.dot_general(a, b, (((1,), (1,)), ((), ())), preferred_element_type=f32)


def nn(a, b):
    return lax.dot_general(a, b, (((1,), (0,)), ((), ())), preferred_element_type=f32)


def small_div(value, by):
    return (value * ((1 << 20) // by + 1)) >> 20


def call(kernel, out_shapes, operands, memory=None, scratch=(), limit=12, hbm=()):
    memory = memory or {}
    many = isinstance(out_shapes, (list, tuple))
    out_specs = [VMEM] * len(out_shapes) if many else VMEM
    operands = [
        pltpu.with_memory_space_constraint(each, pltpu.HBM)
        if at in hbm or memory.get(at) is HBM
        else each
        for at, each in enumerate(operands)
    ]
    return pl.pallas_call(
        kernel,
        out_shape=out_shapes,
        in_specs=[memory.get(at, VMEM) for at in range(len(operands))],
        out_specs=out_specs,
        scratch_shapes=list(scratch),
        compiler_params=pltpu.CompilerParams(vmem_limit_bytes=limit << 20),
    )(*operands)


def norm_kernel(tokens, gain, out):
    parts = []
    for step in range(STEPS):
        widened = tokens[step].astype(f32)
        mean = jnp.mean(widened * widened, axis=-1, keepdims=True)
        parts.append(widened * lax.rsqrt(mean + epsilon) * gain[...])
    both = jnp.concatenate(parts, axis=0).astype(bf16)
    for part in range(N_REP):
        out[part] = both[:, part * COLS : (part + 1) * COLS]


def positions(ids):
    chosen = ids[...]
    expert = lax.broadcasted_iota(jnp.int32, (ALL_ROWS, EXPERTS), 1)
    hits = [chosen[:, which : which + 1] == expert for which in range(TOPK)]
    member = sum(jnp.where(hit, 1.0, 0.0) for hit in hits)
    row = lax.broadcasted_iota(jnp.int32, (ALL_ROWS, ALL_ROWS), 0)
    other = lax.broadcasted_iota(jnp.int32, (ALL_ROWS, ALL_ROWS), 1)
    earlier = (other < row) & (((row >> 2) & 1) == ((other >> 2) & 1))
    position = nn(jnp.where(earlier, 1.0, 0.0).astype(bf16), member.astype(bf16))
    position = jnp.where(member > 0.5, position, 100.0).astype(bf16)
    return hits, jnp.concatenate([position] * Q, axis=0)


WIDE = 256


def split(line):
    target = small_div(line, 2 * CHUNK)
    rest = line - target * (2 * CHUNK)
    step = (rest >= CHUNK).astype(jnp.int32)
    rest = rest - step * CHUNK
    part = small_div(rest, SLOTS)
    slot = rest - part * SLOTS
    local = (slot >= CAP).astype(jnp.int32)
    return target * LOCAL + local, part * 2 + step, (slot - local * CAP).astype(f32)


def send_table_kernel(ids, send):
    _, position = positions(ids)
    column = lax.broadcasted_iota(jnp.int32, (1, Q * ALL_ROWS), 1)
    column = (column >> 6) * 2 + ((column >> 2) & 1)

    def block(index, carry):
        at = pl.multiple_of(index * WIDE, WIDE)
        bucket, piece, place = split(lax.broadcasted_iota(jnp.int32, (WIDE, 1), 0) + at)
        pick = lax.broadcasted_iota(jnp.int32, (WIDE, EXPERTS), 1) == bucket
        found = nt(jnp.where(pick, 1.0, 0.0).astype(bf16), position)
        right = (found == place) & (column == piece)
        send[pl.ds(at, WIDE), :] = jnp.where(right, 1.0, 0.0).astype(bf16)
        return carry

    lax.fori_loop(0, STEPS * N_EP * CHUNK // WIDE, block, 0, unroll=5)


def tables_kernel(ids, weights, keep, sort, unsort):
    hits, position = positions(ids)
    shares = weights[...] / jnp.sum(weights[...], axis=-1, keepdims=True)
    share = sum(
        jnp.where(hit, shares[:, which : which + 1], 0.0) for which, hit in enumerate(hits)
    )
    share = jnp.concatenate([share.astype(bf16)] * Q, axis=0)
    row = lax.broadcasted_iota(jnp.int32, (Q * ALL_ROWS, 1), 0)
    row = (row >> 6) * 2 + ((row >> 2) & 1)

    def keep_block(index, carry):
        at = pl.multiple_of(index * WIDE, WIDE)
        bucket, piece, place = split(lax.broadcasted_iota(jnp.int32, (1, WIDE), 1) + at)
        pick = lax.broadcasted_iota(jnp.int32, (EXPERTS, WIDE), 0) == bucket
        pick = jnp.where(pick, 1.0, 0.0).astype(bf16)
        right = (nn(position, pick) == place) & (row == piece)
        keep[:, pl.ds(at, WIDE)] = jnp.where(right, nn(share, pick), 0.0).astype(bf16)
        return carry

    lax.fori_loop(0, STEPS * N_EP * CHUNK // WIDE, keep_block, 0)

    def stacked_from(line):
        part = small_div(line, 2 * BLOCK)
        rest = line - part * (2 * BLOCK)
        local = (rest >= BLOCK).astype(jnp.int32)
        rest = rest - local * BLOCK
        source = small_div(rest, CAP)
        place = rest - source * CAP
        return source * CHUNK + part * SLOTS + local * CAP + place

    across = stacked_from(lax.broadcasted_iota(jnp.int32, (1, GROUP_ROWS), 1))

    def sort_block(index, carry):
        at = pl.multiple_of(index * LANES, LANES)
        line = lax.broadcasted_iota(jnp.int32, (LANES, 1), 0) + at
        match = lax.broadcasted_iota(jnp.int32, (LANES, GROUP_ROWS), 1) == stacked_from(line)
        sort[pl.ds(at, LANES), :] = jnp.where(match, 1.0, 0.0).astype(bf16)
        unsort[pl.ds(at, LANES), :] = jnp.where(across == line, 1.0, 0.0).astype(bf16)
        return carry

    lax.fori_loop(0, GROUP_ROWS // LANES, sort_block, 0)


def send_kernel(rows, table, out):
    own = rows[...].reshape(ALL_ROWS, COLS)
    stacked = jnp.concatenate(
        [own[:, part * LANES : (part + 1) * LANES] for part in range(Q)], axis=0
    )
    out[...] = nn(table[...], stacked).astype(bf16)


def my_place():
    me = lax.axis_index("rep")
    return me >> 1, me & 1


OFFSETS = ((0, 0), (3, 0), (1, 0), (0, 1), (3, 1), (1, 1), (2, 0), (2, 1))


def slab(ahead):
    x, _ = my_place()
    return pl.ds(pl.multiple_of(((x + ahead) & 3) * (2 * COLS), 2 * COLS), 2 * COLS)


def run_all(copies):
    for copy in copies:
        copy.start()
    for copy in copies:
        copy.wait()


def cut_kernel(aheads, weights, *refs):
    outs, sems = refs[:-1], refs[-1]
    copies = []
    for out, ahead in zip(outs, aheads):
        for local in range(LOCAL):
            for start in range(0, FR, FR // 4):
                rows = pl.ds(start, FR // 4)
                copies.append(
                    pltpu.make_async_copy(
                        weights.at[local, rows, slab(ahead)],
                        out.at[local, rows, :],
                        sems.at[len(copies)],
                    )
                )
    run_all(copies)


def receive_kernel(arrived, table, *outs):
    for step in range(STEPS):
        for group in range(N_EP // GROUP):
            part = arrived[
                group * GROUP : (group + 1) * GROUP, step * CHUNK : (step + 1) * CHUNK, :
            ]
            part = part.astype(f32).reshape(GROUP_ROWS, LANES).astype(bf16)
            sorted_rows = nn(table[...], part).astype(bf16)
            for piece in range(Q):
                for local in range(LOCAL):
                    at = (piece * LOCAL + local) * BLOCK
                    to = local * HALF + group * BLOCK
                    for out, shift in ((outs[step], 0), (outs[2], step * LOCAL * HALF)):
                        out[
                            shift + to : shift + to + BLOCK, piece * LANES : (piece + 1) * LANES
                        ] = sorted_rows[at : at + BLOCK]


def rows_of(refs, local):
    both = []
    for step in range(STEPS):
        if len(refs) == STEPS:
            both.append(refs[step][local * HALF : (local + 1) * HALF, :])
        else:
            at = (step * LOCAL + local) * HALF
            both.append(refs[0][at : at + HALF, :])
    return jnp.concatenate(both, axis=0)


def stage_kernel(all_own, from_before, from_next, from_far, out, sems):
    sources = (all_own.at[:, :, slab(0)], from_before, from_next, from_far)
    run_all(
        [
            pltpu.make_async_copy(source, out.at[index], sems.at[index])
            for index, source in enumerate(sources)
        ]
    )


def chunk_copies(which, gate_all, up_all, gate, up, sems):
    copies = []
    for index, chunk in enumerate(which):
        ahead, aside = OFFSETS[chunk]
        x, y = my_place()
        place = ((x + ahead) & 3) * 2 + (y ^ aside)
        at = pl.ds(pl.multiple_of(place * COLS, COLS), COLS)
        copies.append(
            (
                pltpu.make_async_copy(gate_all.at[:, :, at], gate.at[index], sems.at[0, index]),
                pltpu.make_async_copy(up_all.at[:, :, at], up.at[index], sems.at[1, index]),
            )
        )
    return copies


def add_products(sums, chunk, gate, up):
    for local in range(LOCAL):
        rows = rows_of(chunk, local)
        for which, weights in enumerate((gate, up)):
            at = 2 * local + which
            product = nt(rows, weights[local])
            sums[at] = product if sums[at] is None else sums[at] + product


def take(refs, sizes):
    chunks = []
    for size in sizes:
        chunks.append(refs[:size])
        refs = refs[size:]
    return chunks, refs


def hidden_kernel(which, staged, sizes, *refs):
    chunks, refs = take(refs, sizes)
    sums = [None] * (2 * LOCAL)
    if which[0] > 0:
        sums = [refs[0][at] for at in range(2 * LOCAL)]
        refs = refs[1:]
    gate_all, up_all, total = refs[:3]
    later = refs[3:-3]
    gate, up, sems = refs[-3:]
    count = len(which)
    copies = chunk_copies(which, gate_all, up_all, gate, up, sems)
    if staged:
        copies += chunk_copies(staged, gate_all, up_all, *later, sems.at[:, count:])
    for pair in copies:
        for copy in pair:
            copy.start()
    for index in range(count):
        for copy in copies[index]:
            copy.wait()
        add_products(sums, chunks[index], gate.at[index], up.at[index])
    for at in range(2 * LOCAL):
        total[at] = sums[at]
    for pair in copies[count:]:
        for copy in pair:
            copy.wait()


def late_kernel(sizes, *refs):
    chunks, refs = take(refs, sizes)
    before, gate, up, *outs = refs
    sums = [before[at] for at in range(2 * LOCAL)]
    for index, chunk in enumerate(chunks):
        add_products(sums, chunk, gate.at[index], up.at[index])
    for local in range(LOCAL):
        value = (jax.nn.silu(sums[2 * local]) * sums[2 * local + 1]).astype(bf16)
        for step in range(STEPS):
            outs[step][:, local * FR : (local + 1) * FR] = value[step * HALF : (step + 1) * HALF]


def down_kernel(aside, count, *refs):
    units = [refs[count * index : count * (index + 1)] for index in range(4)]
    staged, out = refs[4 * count :]
    _, y = my_place()
    inside = pl.ds(pl.multiple_of((y ^ aside) * COLS, COLS), COLS)
    sums = [None] * LOCAL
    for index in range(4):
        both = jnp.concatenate([each[...] for each in units[index]], axis=0)
        for local in range(LOCAL):
            product = nn(both[:, local * FR : (local + 1) * FR], staged[index, local, :, inside])
            sums[local] = product if sums[local] is None else sums[local] + product
    for local in range(LOCAL):
        for step in range(count):
            at = (step * LOCAL + local) * HALF
            out[at : at + HALF, :] = sums[local][step * HALF : (step + 1) * HALF].astype(out.dtype)


def return_kernel(mine, other0, other1, table, out):
    for step in range(STEPS):
        for group in range(N_EP // GROUP):
            pieces = []
            for piece in range(Q):
                for local in range(LOCAL):
                    at = local * HALF + group * BLOCK
                    to = step * LOCAL * HALF + at
                    lanes = slice(piece * LANES, (piece + 1) * LANES)
                    other = (other0, other1)[step][at : at + BLOCK, lanes].astype(f32)
                    pieces.append((mine[to : to + BLOCK, lanes] + other).astype(bf16))
            stacked = jnp.concatenate(pieces, axis=0)
            result = nn(table[...], stacked).reshape(GROUP, CHUNK, LANES).astype(bf16)
            out[group * GROUP : (group + 1) * GROUP, step * CHUNK : (step + 1) * CHUNK, :] = result


def mix_kernel(back, keep, out):
    total = nn(keep[...], back[...]).astype(bf16)
    for part in range(Q):
        piece = total[part * ALL_ROWS : (part + 1) * ALL_ROWS]
        out[:, part * LANES : (part + 1) * LANES] = piece


def final_kernel(arrived, out):
    for part in range(N_REP):
        rows = arrived[part].astype(f32)
        for step in range(STEPS):
            out[step, :, part * COLS : (part + 1) * COLS] = rows[
                step * ROWS : (step + 1) * ROWS
            ].astype(bf16)


def rep_index(x, y):
    return (x % 4) * 2 + y % 2


NEXT = [(rep_index(x, y), rep_index(x + 1, y)) for x in range(4) for y in range(2)]
BEFORE = [(rep_index(x, y), rep_index(x - 1, y)) for x in range(4) for y in range(2)]
ACROSS = [(rep_index(x, y), rep_index(x + 2, y)) for x in range(4) for y in range(2)]
BESIDE = [(rep_index(x, y), rep_index(x, y + 1)) for x in range(4) for y in range(2)]


def go(value, pairs):
    return lax.ppermute(value, "rep", pairs)


def swap(value, axis):
    return lax.all_to_all(value, axis, split_axis=0, concat_axis=0, tiled=True)


def gathered(own0, own1, both):
    c = go(both, BESIDE)
    a0 = go(own0, NEXT)
    b1 = go(own1, BEFORE)
    a1 = go(own1, NEXT)
    b0 = go(own0, BEFORE)
    f0 = go(a0, NEXT)
    f1 = go(b1, BEFORE)
    d = go(c, NEXT)
    e = go(c, BEFORE)
    k0 = go(f0, BESIDE)
    k1 = go(f1, BESIDE)
    return ((own0, own1), (a0, a1), (b0, b1), (c,)), ((d,), (e,), (f0, f1), (k0, k1))


def on_device(tokens, norm_gain, expert_ids, route_weights, w_gate, w_up, w_down):
    sds = jax.ShapeDtypeStruct
    normed = call(
        norm_kernel,
        sds((N_REP, STEPS * ROWS, COLS), bf16),
        (tokens.reshape(STEPS, ROWS, D), norm_gain.reshape(1, D)),
        hbm=(0, 1),
    )
    own = swap(normed, "rep")

    def cut(*aheads):
        return call(
            partial(cut_kernel, aheads),
            [sds((LOCAL, FR, 2 * COLS), bf16)] * len(aheads),
            (w_down,),
            memory={0: HBM},
            scratch=[pltpu.SemaphoreType.DMA((8 * len(aheads),))],
        )

    near_next, near_before = cut(1, 3)
    from_before = go(near_next, NEXT)
    from_next = go(near_before, BEFORE)
    from_far = go(cut(2)[0], ACROSS)

    ids = expert_ids.reshape(STEPS, N_REP, ROWS, TOPK).swapaxes(0, 1).reshape(ALL_ROWS, TOPK)
    weights = route_weights.reshape(STEPS, N_REP, ROWS, TOPK).swapaxes(0, 1)
    weights = weights.reshape(ALL_ROWS, TOPK)
    slots = STEPS * N_EP * CHUNK
    send = call(send_table_kernel, sds((slots, Q * ALL_ROWS), bf16), (ids,))
    keep, sort, unsort = call(
        tables_kernel,
        [
            sds((Q * ALL_ROWS, slots), bf16),
            sds((GROUP_ROWS, GROUP_ROWS), bf16),
            sds((GROUP_ROWS, GROUP_ROWS), bf16),
        ],
        (ids, weights),
    )

    outgoing = call(send_kernel, sds((slots, LANES), bf16), (own, send))
    arrived = swap(outgoing.reshape(N_EP, STEPS * CHUNK, LANES), "ep")

    one, two = sds((LOCAL * HALF, COLS), bf16), sds((STEPS * LOCAL * HALF, COLS), bf16)
    rows = call(receive_kernel, [one, one, two], (arrived, sort))
    early, late = gathered(*rows)
    every = (*early, *late)
    total = sds((2 * LOCAL, STEPS * HALF, FR), f32)
    last = (4, 5, 7)
    held = sds((len(last), LOCAL, FR, COLS), bf16)
    sums = ()
    for which, staged in (((0, 1, 2, 3), ()), ((6,), last)):
        parts = [every[index] for index in which]
        count = len(which)
        operands = (*(each for part in parts for each in part), *sums[:1], w_gate, w_up)
        sums = call(
            partial(hidden_kernel, which, staged, tuple(len(part) for part in parts)),
            [total] + [held] * (2 if staged else 0),
            operands,
            memory={len(operands) - 2: HBM, len(operands) - 1: HBM},
            scratch=[
                pltpu.VMEM((count, LOCAL, FR, COLS), bf16),
                pltpu.VMEM((count, LOCAL, FR, COLS), bf16),
                pltpu.SemaphoreType.DMA((2, count + len(staged))),
            ],
            limit=20,
        )
    parts = [every[index] for index in last]
    hidden_all = call(
        partial(late_kernel, tuple(len(part) for part in parts)),
        [sds((HALF, LOCAL * FR), bf16)] * STEPS,
        (*(each for part in parts for each in part), *sums),
    )
    staged = call(
        stage_kernel,
        sds((4, LOCAL, FR, 2 * COLS), bf16),
        (w_down, from_before, from_next, from_far),
        memory={at: HBM for at in range(4)},
        scratch=[pltpu.SemaphoreType.DMA((4,))],
    )
    units = []
    for hidden in hidden_all:
        c = go(hidden, ACROSS)
        a = go(hidden, NEXT)
        b = go(hidden, BEFORE)
        units.append((hidden, a, b, c))

    def down(aside, dtype, *steps):
        count = len(steps)
        chunks = [each for chunk in zip(*steps) for each in chunk]
        return call(
            partial(down_kernel, aside, count),
            sds((count * LOCAL * HALF, COLS), dtype),
            (*chunks, staged),
        )

    others = [go(down(1, bf16, units[step]), BESIDE) for step in range(STEPS)]
    mine = down(0, f32, *units)
    back = call(return_kernel, sds((N_EP, STEPS * CHUNK, LANES), bf16), (mine, *others, unsort))
    back = swap(back, "ep").reshape(slots, LANES)
    mixed = call(mix_kernel, sds((ALL_ROWS, COLS), bf16), (back, keep), hbm=(1,))
    mixed = swap(mixed.reshape(N_REP, STEPS * ROWS, COLS), "rep")
    out = call(final_kernel, sds((STEPS, ROWS, D), bf16), (mixed,))
    return out[:, None, None]


def solution(mesh):
    return jax.shard_map(
        on_device,
        mesh=mesh,
        in_specs=(
            P(None, "ep", "rep", None, None),
            P(),
            P(None, "ep", None, None, None),
            P(None, "ep", None, None, None),
            P("ep", "rep", None),
            P("ep", "rep", None),
            P("ep", "rep", None),
        ),
        out_specs=P(None, "ep", "rep", None, None),
        check_vma=False,
    )
```

```python
from functools import partial

import jax
import jax.numpy as jnp
from jax import lax
from jax.experimental import pallas as pl
from jax.experimental.pallas import tpu as pltpu
from jax.sharding import PartitionSpec as P

epsilon = 1e-06

STEPS = 2
N_REP = 8
N_EP = 32
ROWS = 4
D = 4096
FR = 192
LOCAL = 2
EXPERTS = 64
CAP = 5
TOPK = 8
COLS = D // N_REP
LANES = 128
Q = COLS // LANES
SLOTS = LOCAL * CAP
CHUNK = Q * SLOTS
ALL_ROWS = N_REP * STEPS * ROWS
HALF = N_EP * CAP
GROUP = 16
GROUP_ROWS = GROUP * CHUNK
BLOCK = GROUP * CAP


HBM = pl.BlockSpec(memory_space=pltpu.HBM)
VMEM = pl.BlockSpec(memory_space=pltpu.VMEM)
bf16 = jnp.bfloat16
f32 = jnp.float32


def nt(a, b):
    return lax.dot_general(a, b, (((1,), (1,)), ((), ())), preferred_element_type=f32)


def nn(a, b):
    return lax.dot_general(a, b, (((1,), (0,)), ((), ())), preferred_element_type=f32)


def small_div(value, by):
    return (value * ((1 << 20) // by + 1)) >> 20


def call(kernel, out_shapes, operands, memory=None, scratch=(), limit=12, hbm=()):
    memory = memory or {}
    many = isinstance(out_shapes, (list, tuple))
    out_specs = [VMEM] * len(out_shapes) if many else VMEM
    operands = [
        pltpu.with_memory_space_constraint(each, pltpu.HBM)
        if at in hbm or memory.get(at) is HBM
        else each
        for at, each in enumerate(operands)
    ]
    return pl.pallas_call(
        kernel,
        out_shape=out_shapes,
        in_specs=[memory.get(at, VMEM) for at in range(len(operands))],
        out_specs=out_specs,
        scratch_shapes=list(scratch),
        compiler_params=pltpu.CompilerParams(vmem_limit_bytes=limit << 20),
    )(*operands)


def norm_kernel(tokens, gain, out):
    parts = []
    for step in range(STEPS):
        widened = tokens[step].astype(f32)
        mean = jnp.mean(widened * widened, axis=-1, keepdims=True)
        parts.append(widened * lax.rsqrt(mean + epsilon) * gain[...])
    both = jnp.concatenate(parts, axis=0).astype(bf16)
    for part in range(N_REP):
        out[part] = both[:, part * COLS : (part + 1) * COLS]


def by_place(ref):
    return jnp.concatenate(
        [ref[step, place] for place in range(N_REP) for step in range(STEPS)], axis=0
    )


def positions(ids):
    chosen = by_place(ids)
    expert = lax.broadcasted_iota(jnp.int32, (ALL_ROWS, EXPERTS), 1)
    hits = [chosen[:, which : which + 1] == expert for which in range(TOPK)]
    member = sum(jnp.where(hit, 1.0, 0.0) for hit in hits)
    row = lax.broadcasted_iota(jnp.int32, (ALL_ROWS, ALL_ROWS), 0)
    other = lax.broadcasted_iota(jnp.int32, (ALL_ROWS, ALL_ROWS), 1)
    earlier = (other < row) & (((row >> 2) & 1) == ((other >> 2) & 1))
    position = nn(jnp.where(earlier, 1.0, 0.0).astype(bf16), member.astype(bf16))
    position = jnp.where(member > 0.5, position, 100.0).astype(bf16)
    return hits, jnp.concatenate([position] * Q, axis=0)


WIDE = 256


def split(line):
    target = small_div(line, 2 * CHUNK)
    rest = line - target * (2 * CHUNK)
    step = (rest >= CHUNK).astype(jnp.int32)
    rest = rest - step * CHUNK
    part = small_div(rest, SLOTS)
    slot = rest - part * SLOTS
    local = (slot >= CAP).astype(jnp.int32)
    return target * LOCAL + local, part * 2 + step, (slot - local * CAP).astype(f32)


def send_table_kernel(ids, send):
    _, position = positions(ids)
    column = lax.broadcasted_iota(jnp.int32, (1, Q * ALL_ROWS), 1)
    column = (column >> 6) * 2 + ((column >> 2) & 1)

    def block(index, carry):
        at = pl.multiple_of(index * WIDE, WIDE)
        bucket, piece, place = split(lax.broadcasted_iota(jnp.int32, (WIDE, 1), 0) + at)
        pick = lax.broadcasted_iota(jnp.int32, (WIDE, EXPERTS), 1) == bucket
        found = nt(jnp.where(pick, 1.0, 0.0).astype(bf16), position)
        right = (found == place) & (column == piece)
        send[pl.ds(at, WIDE), :] = jnp.where(right, 1.0, 0.0).astype(bf16)
        return carry

    lax.fori_loop(0, STEPS * N_EP * CHUNK // WIDE, block, 0, unroll=5)


def tables_kernel(ids, weights, keep, sort, unsort):
    hits, position = positions(ids)
    shares = by_place(weights)
    shares = shares / jnp.sum(shares, axis=-1, keepdims=True)
    share = sum(
        jnp.where(hit, shares[:, which : which + 1], 0.0) for which, hit in enumerate(hits)
    )
    share = jnp.concatenate([share.astype(bf16)] * Q, axis=0)
    row = lax.broadcasted_iota(jnp.int32, (Q * ALL_ROWS, 1), 0)
    row = (row >> 6) * 2 + ((row >> 2) & 1)

    def keep_block(index, carry):
        at = pl.multiple_of(index * WIDE, WIDE)
        bucket, piece, place = split(lax.broadcasted_iota(jnp.int32, (1, WIDE), 1) + at)
        pick = lax.broadcasted_iota(jnp.int32, (EXPERTS, WIDE), 0) == bucket
        pick = jnp.where(pick, 1.0, 0.0).astype(bf16)
        right = (nn(position, pick) == place) & (row == piece)
        keep[:, pl.ds(at, WIDE)] = jnp.where(right, nn(share, pick), 0.0).astype(bf16)
        return carry

    lax.fori_loop(0, STEPS * N_EP * CHUNK // WIDE, keep_block, 0)

    def stacked_from(line):
        part = small_div(line, 2 * BLOCK)
        rest = line - part * (2 * BLOCK)
        local = (rest >= BLOCK).astype(jnp.int32)
        rest = rest - local * BLOCK
        source = small_div(rest, CAP)
        place = rest - source * CAP
        return source * CHUNK + part * SLOTS + local * CAP + place

    across = stacked_from(lax.broadcasted_iota(jnp.int32, (1, GROUP_ROWS), 1))

    def sort_block(index, carry):
        at = pl.multiple_of(index * LANES, LANES)
        line = lax.broadcasted_iota(jnp.int32, (LANES, 1), 0) + at
        match = lax.broadcasted_iota(jnp.int32, (LANES, GROUP_ROWS), 1) == stacked_from(line)
        sort[pl.ds(at, LANES), :] = jnp.where(match, 1.0, 0.0).astype(bf16)
        unsort[pl.ds(at, LANES), :] = jnp.where(across == line, 1.0, 0.0).astype(bf16)
        return carry

    lax.fori_loop(0, GROUP_ROWS // LANES, sort_block, 0)


def send_kernel(rows, table, out):
    own = rows[...].reshape(ALL_ROWS, COLS)
    stacked = jnp.concatenate(
        [own[:, part * LANES : (part + 1) * LANES] for part in range(Q)], axis=0
    )
    out[...] = nn(table[...], stacked).astype(bf16)


def my_place():
    me = lax.axis_index("rep")
    return me >> 1, me & 1


OFFSETS = ((0, 0), (3, 0), (1, 0), (0, 1), (3, 1), (1, 1), (2, 0), (2, 1))


def slab(ahead):
    x, _ = my_place()
    return pl.ds(pl.multiple_of(((x + ahead) & 3) * (2 * COLS), 2 * COLS), 2 * COLS)


def run_all(copies):
    for copy in copies:
        copy.start()
    for copy in copies:
        copy.wait()


def cut_copies(aheads, weights, outs, sems):
    return [
        pltpu.make_async_copy(weights.at[:, :, slab(ahead)], out, sems.at[index])
        for index, (ahead, out) in enumerate(zip(aheads, outs))
    ]


def far_kernel(weights, out, sems):
    run_all(cut_copies((2,), weights, (out,), sems))


def near_kernel(weights, all_ids, near_next, near_before, send, ids, sems):
    copies = cut_copies((1, 3), weights, (near_next, near_before), sems)
    fetch = pltpu.make_async_copy(all_ids, ids, sems.at[2])
    fetch.start()
    for copy in copies:
        copy.start()
    fetch.wait()
    send_table_kernel(ids, send)
    for copy in copies:
        copy.wait()


def receive_kernel(arrived, table, *outs):
    for step in range(STEPS):
        for group in range(N_EP // GROUP):
            part = arrived[
                group * GROUP : (group + 1) * GROUP, step * CHUNK : (step + 1) * CHUNK, :
            ]
            part = part.astype(f32).reshape(GROUP_ROWS, LANES).astype(bf16)
            sorted_rows = nn(table[...], part).astype(bf16)
            for piece in range(Q):
                for local in range(LOCAL):
                    at = (piece * LOCAL + local) * BLOCK
                    to = local * HALF + group * BLOCK
                    for out, shift in ((outs[step], 0), (outs[2], step * LOCAL * HALF)):
                        out[
                            shift + to : shift + to + BLOCK, piece * LANES : (piece + 1) * LANES
                        ] = sorted_rows[at : at + BLOCK]


def rows_of(refs, local):
    both = []
    for step in range(STEPS):
        if len(refs) == STEPS:
            both.append(refs[step][local * HALF : (local + 1) * HALF, :])
        else:
            at = (step * LOCAL + local) * HALF
            both.append(refs[0][at : at + HALF, :])
    return jnp.concatenate(both, axis=0)


def stage_kernel(all_own, from_before, from_next, from_far, out, sems):
    sources = (all_own.at[:, :, slab(0)], from_before, from_next, from_far)
    run_all(
        [
            pltpu.make_async_copy(source, out.at[index], sems.at[index])
            for index, source in enumerate(sources)
        ]
    )


def chunk_copies(which, gate_all, up_all, gate, up, sems):
    copies = []
    for index, chunk in enumerate(which):
        ahead, aside = OFFSETS[chunk]
        x, y = my_place()
        place = ((x + ahead) & 3) * 2 + (y ^ aside)
        at = pl.ds(pl.multiple_of(place * COLS, COLS), COLS)
        copies.append(
            (
                pltpu.make_async_copy(gate_all.at[:, :, at], gate.at[index], sems.at[0, index]),
                pltpu.make_async_copy(up_all.at[:, :, at], up.at[index], sems.at[1, index]),
            )
        )
    return copies


def add_products(sums, chunk, gate, up):
    for local in range(LOCAL):
        rows = rows_of(chunk, local)
        for which, weights in enumerate((gate, up)):
            at = 2 * local + which
            product = nt(rows, weights[local])
            sums[at] = product if sums[at] is None else sums[at] + product


def take(refs, sizes):
    chunks = []
    for size in sizes:
        chunks.append(refs[:size])
        refs = refs[size:]
    return chunks, refs


def hidden_kernel(which, staged, sizes, *refs):
    chunks, refs = take(refs, sizes)
    sums = [None] * (2 * LOCAL)
    if which[0] > 0:
        sums = [refs[0][at] for at in range(2 * LOCAL)]
        refs = refs[1:]
    gate_all, up_all, total = refs[:3]
    later = refs[3:-3]
    gate, up, sems = refs[-3:]
    count = len(which)
    copies = chunk_copies(which, gate_all, up_all, gate, up, sems)
    if staged:
        copies += chunk_copies(staged, gate_all, up_all, *later, sems.at[:, count:])
    for pair in copies:
        for copy in pair:
            copy.start()
    for index in range(count):
        for copy in copies[index]:
            copy.wait()
        add_products(sums, chunks[index], gate.at[index], up.at[index])
    for at in range(2 * LOCAL):
        total[at] = sums[at]
    for pair in copies[count:]:
        for copy in pair:
            copy.wait()


def late_kernel(sizes, *refs):
    chunks, refs = take(refs, sizes)
    before, gate, up, *outs = refs
    sums = [before[at] for at in range(2 * LOCAL)]
    for index, chunk in enumerate(chunks):
        add_products(sums, chunk, gate.at[index], up.at[index])
    for local in range(LOCAL):
        value = (jax.nn.silu(sums[2 * local]) * sums[2 * local + 1]).astype(bf16)
        for step in range(STEPS):
            outs[step][:, local * FR : (local + 1) * FR] = value[step * HALF : (step + 1) * HALF]


def down_kernel(aside, count, *refs):
    units = [refs[count * index : count * (index + 1)] for index in range(4)]
    staged, out = refs[4 * count :]
    _, y = my_place()
    inside = pl.ds(pl.multiple_of((y ^ aside) * COLS, COLS), COLS)
    sums = [None] * LOCAL
    for index in range(4):
        both = jnp.concatenate([each[...] for each in units[index]], axis=0)
        for local in range(LOCAL):
            product = nn(both[:, local * FR : (local + 1) * FR], staged[index, local, :, inside])
            sums[local] = product if sums[local] is None else sums[local] + product
    for local in range(LOCAL):
        for step in range(count):
            at = (step * LOCAL + local) * HALF
            out[at : at + HALF, :] = sums[local][step * HALF : (step + 1) * HALF].astype(out.dtype)


def return_kernel(mine, other0, other1, table, out):
    for step in range(STEPS):
        for group in range(N_EP // GROUP):
            pieces = []
            for piece in range(Q):
                for local in range(LOCAL):
                    at = local * HALF + group * BLOCK
                    to = step * LOCAL * HALF + at
                    lanes = slice(piece * LANES, (piece + 1) * LANES)
                    other = (other0, other1)[step][at : at + BLOCK, lanes].astype(f32)
                    pieces.append((mine[to : to + BLOCK, lanes] + other).astype(bf16))
            stacked = jnp.concatenate(pieces, axis=0)
            result = nn(table[...], stacked).reshape(GROUP, CHUNK, LANES).astype(bf16)
            out[group * GROUP : (group + 1) * GROUP, step * CHUNK : (step + 1) * CHUNK, :] = result


def mix_kernel(back, keep, out):
    total = nn(keep[...], back[...]).astype(bf16)
    for part in range(Q):
        piece = total[part * ALL_ROWS : (part + 1) * ALL_ROWS]
        out[:, part * LANES : (part + 1) * LANES] = piece


def final_kernel(arrived, out):
    for part in range(N_REP):
        rows = arrived[part].astype(f32)
        for step in range(STEPS):
            out[step, :, part * COLS : (part + 1) * COLS] = rows[
                step * ROWS : (step + 1) * ROWS
            ].astype(bf16)


def rep_index(x, y):
    return (x % 4) * 2 + y % 2


NEXT = [(rep_index(x, y), rep_index(x + 1, y)) for x in range(4) for y in range(2)]
BEFORE = [(rep_index(x, y), rep_index(x - 1, y)) for x in range(4) for y in range(2)]
ACROSS = [(rep_index(x, y), rep_index(x + 2, y)) for x in range(4) for y in range(2)]
BESIDE = [(rep_index(x, y), rep_index(x, y + 1)) for x in range(4) for y in range(2)]


def go(value, pairs):
    return lax.ppermute(value, "rep", pairs)


def swap(value, axis):
    return lax.all_to_all(value, axis, split_axis=0, concat_axis=0, tiled=True)


def gathered(own0, own1, both):
    c = go(both, BESIDE)
    a0 = go(own0, NEXT)
    b1 = go(own1, BEFORE)
    a1 = go(own1, NEXT)
    b0 = go(own0, BEFORE)
    f0 = go(a0, NEXT)
    f1 = go(b1, BEFORE)
    d = go(c, NEXT)
    e = go(c, BEFORE)
    k0 = go(f0, BESIDE)
    k1 = go(f1, BESIDE)
    return ((own0, own1), (a0, a1), (b0, b1), (c,)), ((d,), (e,), (f0, f1), (k0, k1))


def on_device(tokens, norm_gain, expert_ids, route_weights, w_gate, w_up, w_down):
    sds = jax.ShapeDtypeStruct
    normed = call(
        norm_kernel,
        sds((N_REP, STEPS * ROWS, COLS), bf16),
        (tokens.reshape(STEPS, ROWS, D), norm_gain.reshape(1, D)),
        hbm=(0, 1),
    )
    own = swap(normed, "rep")

    ids = expert_ids.reshape(STEPS, N_REP, ROWS, TOPK)
    weights = route_weights.reshape(STEPS, N_REP, ROWS, TOPK)
    slots = STEPS * N_EP * CHUNK
    part = sds((LOCAL, FR, 2 * COLS), bf16)
    near_next, near_before, send = call(
        near_kernel,
        [part, part, sds((slots, Q * ALL_ROWS), bf16)],
        (w_down, ids),
        memory={0: HBM, 1: HBM},
        scratch=[
            pltpu.VMEM((STEPS, N_REP, ROWS, TOPK), jnp.int32),
            pltpu.SemaphoreType.DMA((3,)),
        ],
    )
    far = call(
        far_kernel, part, (w_down,), memory={0: HBM}, scratch=[pltpu.SemaphoreType.DMA((1,))]
    )
    from_before = go(near_next, NEXT)
    from_next = go(near_before, BEFORE)
    from_far = go(far, ACROSS)
    keep, sort, unsort = call(
        tables_kernel,
        [
            sds((Q * ALL_ROWS, slots), bf16),
            sds((GROUP_ROWS, GROUP_ROWS), bf16),
            sds((GROUP_ROWS, GROUP_ROWS), bf16),
        ],
        (ids, weights),
    )

    outgoing = call(send_kernel, sds((slots, LANES), bf16), (own, send))
    arrived = swap(outgoing.reshape(N_EP, STEPS * CHUNK, LANES), "ep")

    one, two = sds((LOCAL * HALF, COLS), bf16), sds((STEPS * LOCAL * HALF, COLS), bf16)
    rows = call(receive_kernel, [one, one, two], (arrived, sort))
    early, late = gathered(*rows)
    every = (*early, *late)
    total = sds((2 * LOCAL, STEPS * HALF, FR), f32)
    last = (4, 5, 7)
    held = sds((len(last), LOCAL, FR, COLS), bf16)
    sums = ()
    for which, staged in (((0, 1, 2, 3), ()), ((6,), last)):
        parts = [every[index] for index in which]
        count = len(which)
        operands = (*(each for part in parts for each in part), *sums[:1], w_gate, w_up)
        sums = call(
            partial(hidden_kernel, which, staged, tuple(len(part) for part in parts)),
            [total] + [held] * (2 if staged else 0),
            operands,
            memory={len(operands) - 2: HBM, len(operands) - 1: HBM},
            scratch=[
                pltpu.VMEM((count, LOCAL, FR, COLS), bf16),
                pltpu.VMEM((count, LOCAL, FR, COLS), bf16),
                pltpu.SemaphoreType.DMA((2, count + len(staged))),
            ],
            limit=20,
        )
    parts = [every[index] for index in last]
    hidden_all = call(
        partial(late_kernel, tuple(len(part) for part in parts)),
        [sds((HALF, LOCAL * FR), bf16)] * STEPS,
        (*(each for part in parts for each in part), *sums),
    )
    staged = call(
        stage_kernel,
        sds((4, LOCAL, FR, 2 * COLS), bf16),
        (w_down, from_before, from_next, from_far),
        memory={at: HBM for at in range(4)},
        scratch=[pltpu.SemaphoreType.DMA((4,))],
    )
    units = []
    for hidden in hidden_all:
        c = go(hidden, ACROSS)
        a = go(hidden, NEXT)
        b = go(hidden, BEFORE)
        units.append((hidden, a, b, c))

    def down(aside, dtype, *steps):
        count = len(steps)
        chunks = [each for chunk in zip(*steps) for each in chunk]
        return call(
            partial(down_kernel, aside, count),
            sds((count * LOCAL * HALF, COLS), dtype),
            (*chunks, staged),
        )

    others = [go(down(1, bf16, units[step]), BESIDE) for step in range(STEPS)]
    mine = down(0, f32, *units)
    back = call(return_kernel, sds((N_EP, STEPS * CHUNK, LANES), bf16), (mine, *others, unsort))
    back = swap(back, "ep").reshape(slots, LANES)
    mixed = call(mix_kernel, sds((ALL_ROWS, COLS), bf16), (back, keep))
    mixed = swap(mixed.reshape(N_REP, STEPS * ROWS, COLS), "rep")
    out = call(final_kernel, sds((STEPS, ROWS, D), bf16), (mixed,))
    return out[:, None, None]


def solution(mesh):
    return jax.shard_map(
        on_device,
        mesh=mesh,
        in_specs=(
            P(None, "ep", "rep", None, None),
            P(),
            P(None, "ep", None, None, None),
            P(None, "ep", None, None, None),
            P("ep", "rep", None),
            P("ep", "rep", None),
            P("ep", "rep", None),
        ),
        out_specs=P(None, "ep", "rep", None, None),
        check_vma=False,
    )
```
